32 devices in a mesh: grp: 2 (over y), row: 4 (over x, core), col: 4 (over z).
Axes of the slice: x: 2, y: 2, z: 4, core: 2. Of those that a mesh axis runs over, the one named last changes fastest.
Arguments:
- features: bfloat16 [32, 1024, 1024], P(None, ('grp', 'row'), 'col'), parts along dimension 1, may hold values from -6 to 6
- conv_weight: bfloat16 [32, 3, 3], replicated, may hold values from -0.375 to 0.375
- row_taps: float32 [8, 2, 33], replicated, may hold values from -1 to 1
- col_taps: float32 [8, 2, 33], replicated, may hold values from -1 to 1
- kernel_weight: float32 [8], replicated, may hold values from 0.1 to 1
- target: float32 [1024, 1024], P(('grp', 'row'), 'col'), parts along dimension 0, may hold values from 0 to 1
- block_list: int32 [8, 4, 8], P(('grp', 'row'), 'col'), parts along dimension 0, may hold values from 0 to 8, as said below
Outputs:
- grad_weight: float32 [64, 3, 3], P('grp'), parts along dimension 0
- grad_features: bfloat16 [32, 1024, 1024], P(None, ('grp', 'row'), 'col'), parts along dimension 1
The draws below stay inside these ranges and needn't reach their ends.
There are 2 independent parts, one for each index of `grp`. The reference program is written for one: setup_inputs(seed, part) draws one part's arguments, and reference() takes and returns one part's arrays. A program takes and returns all parts, laid end to end along the dimension named above; an argument that names none is the same for every part. Nothing has to cross between parts.
Inputs may be any that keep to these rules, and one draw needn't show every extreme that they name: `block_list`: each tile's entry lists its occupied blocks in increasing order, then entries equal to 8; every tile has at least one occupied block, and in every draw some tile has all 8 occupied.
All inputs are finite; a program needn't handle non-finite values.
Results may differ from the reference program's by a relative error of at most 0.0004.
Values may be sent and summed in bfloat16 or wider, within the bound.
No kernel may reach another device: no remote copies, remote signals or barrier semaphores. Data moves between devices by JAX's collectives and lax.ppermute only.
A program may use at most 128 MiB of HBM per device.

```python
import math
import jax
import jax.numpy as jnp
from jax import lax

CH = 32
KERN = 8
HALF = 16
TAPS = 33
BLOCK = 64
W = 1024
H = 512
GRID_R = 4
GRID_C = 4
TILE_R = 128
TILE_C = 256
NB = 8


def draw_block_list(key, part):
    key_one, key_two, key_three, key_four = jax.random.split(key, 4)
    tile_total = GRID_R * GRID_C
    first_pick = jax.random.randint(key_one, (tile_total,), 1, NB + 1)
    second_pick = jax.random.randint(key_two, (tile_total,), 1, NB + 1)
    listed_count = jnp.minimum(first_pick, second_pick)
    full_tile = jax.random.randint(key_three, (), 0, tile_total)
    listed_count = jnp.where(jnp.arange(tile_total) == full_tile, NB, listed_count)
    positions = jnp.arange(NB, dtype=jnp.int32)
    scores = jax.random.randint(key_four, (tile_total, NB), 0, 1 << 20) * NB + positions[None, :]
    rank_order = jnp.argsort(jnp.argsort(scores, axis=1), axis=1)
    chosen = rank_order < listed_count[:, None]
    sort_keys = jnp.where(chosen, positions[None, :], NB + positions[None, :])
    sorted_ids = jnp.argsort(sort_keys, axis=1).astype(jnp.int32)
    result = jnp.where(positions[None, :] < listed_count[:, None], sorted_ids, NB)
    return result.reshape(GRID_R, GRID_C, NB).astype(jnp.int32)


def steps_of(stream_key, extent, cuts, least, largest):
    factor_of, own = 1.0, jax.random.fold_in(stream_key, 6)
    for dim, parts in cuts:
        draws = jnp.exp(jax.random.uniform(jax.random.fold_in(own, dim), (parts,), jnp.float32, least / len(cuts), largest / len(cuts)))
        factor_of = factor_of * jnp.repeat(draws, extent[dim] // parts).reshape([-1 if axis == dim else 1 for axis in range(len(extent))])
    return factor_of


def bell_draw(rng, extent, scale, limit, cuts=(), kind=jnp.bfloat16):
    drawn = jax.random.normal(rng, extent, jnp.float32) * scale
    if len(cuts) > 0:
        drawn = steps_of(rng, extent, cuts, -0.22, 0.18) * drawn
    return jnp.clip(drawn, min=-limit, max=limit).astype(kind)


def setup_inputs(seed: int = 0, part: int = 0) -> dict:
    keys = jax.random.split(jax.random.key(seed), 8)
    part_keys = jax.random.split(jax.random.fold_in(keys[7], part), 8)
    return {
        "features": bell_draw(part_keys[0], (CH, H, W), 1.0, 6.0, ((1, 4), (2, 4))),
        "conv_weight": bell_draw(keys[1], (CH, 3, 3), (CH * 9) ** -0.5, 0.375),
        "row_taps": bell_draw(keys[2], (KERN, 2, TAPS), TAPS ** -0.5, 1.0, (), jnp.float32),
        "col_taps": bell_draw(keys[3], (KERN, 2, TAPS), TAPS ** -0.5, 1.0, (), jnp.float32),
        "kernel_weight": jnp.clip(jnp.exp(jax.random.uniform(keys[4], (KERN,), jnp.float32, math.log(0.1), math.log(1.0))), 0.1, 1.0),
        "target": jnp.clip(1.0 * jax.random.uniform(part_keys[5], (H, W), jnp.float32) ** steps_of(part_keys[5], (H, W), ((0, 4), (1, 4)), -0.2, 0.2), 0.0, 1.0),
        "block_list": draw_block_list(jax.random.fold_in(jax.random.fold_in(keys[7], part), 71), part),
    }


HIGH = lax.Precision.HIGHEST

def occupancy(block_list):
    blocks_r = TILE_R // BLOCK
    blocks_c = TILE_C // BLOCK
    named = (block_list[:, :, :, None] == jnp.arange(NB)[None, None, None, :]).any(2)
    block_grid = named.astype(jnp.float32).reshape(GRID_R, GRID_C, blocks_r, blocks_c)
    block_grid = block_grid.transpose(0, 2, 1, 3).reshape(GRID_R * blocks_r, GRID_C * blocks_c)
    return jnp.repeat(jnp.repeat(block_grid, BLOCK, 0), BLOCK, 1)

def aerial_image(mask, row_taps, col_taps, kernel_weight):
    filters = 2 * KERN
    row_kernel = row_taps.reshape(filters, 1, TAPS, 1)
    col_kernel = col_taps.reshape(filters, 1, 1, TAPS)
    rowed = lax.conv_general_dilated(mask[None, None], row_kernel, (1, 1), ((HALF, HALF), (0, 0)), precision=HIGH)
    optic_field = lax.conv_general_dilated(rowed, col_kernel, (1, 1), ((0, 0), (HALF, HALF)), feature_group_count=filters, precision=HIGH)[0]
    weights = jnp.repeat(kernel_weight, 2)
    return jnp.einsum('f,fhw->hw', weights, optic_field * optic_field, precision=HIGH)

def reference(features, conv_weight, row_taps, col_taps, kernel_weight, target, block_list):
    occupied = occupancy(block_list)

    def objective(weight_f32, feats_f32):
        logits = lax.conv_general_dilated(feats_f32[None], weight_f32[None], (1, 1), ((1, 1), (1, 1)), precision=HIGH)[0, 0]
        mask = occupied * jax.nn.sigmoid(logits)
        aerial = aerial_image(mask, row_taps, col_taps, kernel_weight)
        mismatch = aerial - target
        return 0.5 * jnp.sum(mismatch * mismatch)
    weight_f32 = conv_weight.astype(jnp.float32)
    feats_f32 = features.astype(jnp.float32)
    loss_value, pullback = jax.vjp(objective, weight_f32, feats_f32)
    grad_w, grad_f = pullback(jnp.ones((), loss_value.dtype))
    return (grad_w / math.sqrt(H * W), grad_f.astype(jnp.bfloat16))
```

```python
import functools
import math

import jax
import jax.numpy as jnp
from jax import lax
from jax.experimental import pallas as pl
from jax.experimental.pallas import tpu as pltpu
from jax.sharding import PartitionSpec as P

BLOCK = 64
ROWS = 16
WIN = 32
MIB = 1 << 20
F32 = jnp.float32
BF16 = jnp.bfloat16


def up(value, multiple):
    return -(-value // multiple) * multiple


def iota(shape, dim):
    return lax.broadcasted_iota(jnp.int32, shape, dim)


def split(value):
    high = value.astype(BF16)
    return high, (value - high.astype(F32)).astype(BF16)


def dot(left, right, dims=((1,), (0,)), precision=None):
    return lax.dot_general(
        left, right, (dims, ((), ())), precision=precision, preferred_element_type=F32
    )


NT = ((1,), (1,))


class Sizes:
    def __init__(self, channels, tile_rows, tile_cols, taps, filters):
        self.channels, self.rows, self.cols = channels, tile_rows, tile_cols
        self.taps, self.filters = taps, filters
        self.half = (taps - 1) // 2
        self.mask_halo = 2 * self.half + 1
        self.field_halo = self.half + 1
        self.strip = self.mask_halo + 1
        self.base = self.mask_halo - 1
        self.width = up(tile_cols + 2 * self.mask_halo, 128)
        self.field_rows = tile_rows + 2 * self.field_halo
        self.field_cols = tile_cols + 2 * self.field_halo
        self.field_pad = up(self.field_rows, 16)
        self.grad_pad = tile_rows + ROWS
        mask_rows = tile_rows + 2 * self.mask_halo
        self.depth = up(max(mask_rows, self.field_pad + taps), 128)
        self.steps = tile_rows // ROWS
        self.strip_rows = up(self.strip + 1 + self.field_halo, 8)
        self.fold = self.grad_pad // 2


def band_kernel(s, row_taps, col_taps, kernel_weight, row_high, row_low, col_fwd, col_adj, adj_high, adj_low, flipped):
    for f in range(s.filters):
        k, p = f // 2, f % 2
        pad = jnp.zeros((1, s.depth - s.taps), F32)
        row = jnp.concatenate([row_taps[k, p : p + 1, :], pad], 1)
        col = jnp.concatenate([col_taps[k, p : p + 1, :], pad], 1)
        band = pltpu.roll(
            jnp.broadcast_to(row, (s.field_pad, s.depth)), 0, 1, stride=1, stride_axis=0
        )
        row_high[f], row_low[f] = split(band)
        turned = pltpu.roll(
            jnp.broadcast_to(row * (2.0 * kernel_weight[k]), (s.field_pad, s.depth)),
            s.depth - (s.taps - 1),
            1,
            stride=1,
            stride_axis=0,
        )
        flipped[f * s.field_pad : (f + 1) * s.field_pad, :] = turned
        wide = col[:, :256]
        band = pltpu.roll(jnp.broadcast_to(wide, (128, 256)), 0, 1, stride=1, stride_axis=0)
        col_fwd[f, :128, :], col_fwd[f, 128:, :] = split(band)
        band = pltpu.roll(
            jnp.broadcast_to(wide, (256, 256)), 256 - (s.taps - 1), 1, stride=1, stride_axis=0
        )
        col_adj[f, :, :128], col_adj[f, :, 128:] = split(band[:, :128])
    turned = flipped[...].T[: s.grad_pad, :]
    adj_high[...], adj_low[...] = split(turned)


def edge_kernel(s, listed, features, conv_weight, target, table, partial, left_out, right_out, acc):
    lanes = 6 * WIN
    u, lane = iota((ROWS, 256), 0), iota((ROWS, 256), 1)
    h, b = lane % WIN, (lane // WIN) % 3
    taps = conv_weight[...].astype(F32)
    total = jnp.zeros((s.channels, ROWS, 256), F32)
    for row_shift in range(3):
        for col_shift in range(3):
            hit = (h == u - row_shift + 2) & (b == col_shift) & (lane < lanes)
            total += taps[:, row_shift : row_shift + 1, col_shift : col_shift + 1] * jnp.where(
                hit, 1.0, 0.0
            )
    flat = total.reshape(s.channels * ROWS, 256)
    table[...] = flat.astype(BF16)
    left = flat[:, :128].T[: 3 * WIN].astype(BF16)
    acc[...] = jnp.zeros_like(acc)
    for k in range(s.steps):
        block = features[:, k * ROWS : (k + 1) * ROWS, :].reshape(s.channels * ROWS, s.cols)
        sums = dot(left, block)
        for b in range(3):
            acc[b, k * ROWS : k * ROWS + WIN, :] += sums[b * WIN : (b + 1) * WIN]
    whole = jnp.zeros((s.grad_pad, s.width), F32)
    blank = jnp.zeros((s.grad_pad, s.width - s.cols), F32)
    for b in range(3):
        part = jnp.concatenate([acc[b, : s.grad_pad], blank], 1)
        whole += pltpu.roll(part, s.base + 2 - b, 1)
    partial[...] = whole

    place, row = iota((s.grad_pad, 128), 1), iota((s.grad_pad, 128), 0)
    aim = jnp.concatenate([target[...], jnp.zeros((s.grad_pad - s.rows, s.cols), F32)], 0)
    aim = jnp.concatenate([aim, jnp.zeros((s.grad_pad, s.width - s.cols), F32)], 1)
    across = s.cols // BLOCK
    for out, first, first_aim, block_col in (
        (left_out, s.base, 0, 0),
        (right_out, s.cols, s.cols - s.field_halo, across - 1),
    ):
        logits = pltpu.roll(whole, (s.width - first) % s.width, 1)[:, :128]
        wanted = pltpu.roll(aim, (s.width - first_aim + s.strip) % s.width, 1)[:, :128]
        number = (row // BLOCK) * across + block_col
        used = jnp.zeros((s.grad_pad, 128), F32)
        for n in range(listed.shape[2]):
            used = jnp.where(number == listed[0, 0, n], 1.0, used)
        used = jnp.where(row < s.rows, used, 0.0)
        value = jnp.where(place < s.strip, logits, wanted)
        value = jnp.where(place < s.strip + s.field_halo, value, used)
        value = jnp.where(place < s.strip + s.field_halo + 1, value, 0.0)
        out[...] = jnp.where(
            iota((s.fold, 128), 1) < 64, value[: s.fold], pltpu.roll(value[s.fold :], 64, 1)
        )


def unfolded(s, ref):
    value = ref[...]
    low = iota((s.fold, 128), 1) < 64
    return jnp.concatenate(
        [jnp.where(low, value, 0.0), jnp.where(low, pltpu.roll(value, 64, 1), 0.0)], 0
    )


def middle_kernel(s, sides, listed, partial, target, from_left, from_right, logits, aim, occupied, up_out, down_out):
    extra = jnp.zeros((s.grad_pad, s.width - 128), F32)
    lane = iota((s.grad_pad, 128), 1)
    has_left, has_right = sides[0], sides[1]
    west = jnp.where(has_left > 0, unfolded(s, from_left), 0.0)
    east = jnp.where(has_right > 0, unfolded(s, from_right), 0.0)

    def placed(value, keep_from, keep, offset):
        kept = jnp.where((lane >= keep_from) & (lane < keep_from + keep), value, 0.0)
        wide = jnp.concatenate([kept, extra], 1)
        return pltpu.roll(wide, (offset - keep_from) % s.width, 1)

    whole = partial[...] + placed(west, 0, s.strip, 0)
    whole += placed(east, 0, s.strip, s.cols + s.base)
    logits[...] = whole
    own = jnp.concatenate([target[...], jnp.zeros((s.rows, s.width - s.cols), F32)], 1)
    aims = pltpu.roll(own, s.field_halo, 1)
    aims += placed(west, s.strip, s.field_halo, 0)[: s.rows]
    aims += placed(east, s.strip, s.field_halo, s.cols + s.field_halo)[: s.rows]
    aim[...] = aims

    across, down = s.cols // BLOCK, s.rows // BLOCK
    row, col = iota((8, s.width), 0), iota((8, s.width), 1) - s.mask_halo
    inside = (col >= 0) & (col < s.cols) & (row < down)
    number = jnp.where(inside, row * across + (col + BLOCK) // BLOCK - 1, -1)
    used = jnp.zeros((8, s.width), F32)
    for n in range(listed.shape[2]):
        used = jnp.where(number == listed[0, 0, n], 1.0, used)
    flag = s.strip + s.field_halo
    for r in range(down):
        here = row == r
        used = jnp.where(here & (col < 0), west[r * BLOCK : r * BLOCK + 1, flag : flag + 1], used)
        beyond = here & (col >= s.cols) & (col < s.cols + s.mask_halo)
        used = jnp.where(beyond, east[r * BLOCK : r * BLOCK + 1, flag : flag + 1], used)
    occupied[...] = used

    for out, first, first_aim, block_row in (
        (up_out, 0, 0, 0),
        (down_out, s.rows + 2 - s.strip, s.rows - s.field_halo, down - 1),
    ):
        out[...] = jnp.zeros_like(out)
        out[: s.strip, :] = whole[first : first + s.strip]
        out[s.strip : s.strip + 1, :] = used[block_row : block_row + 1]
        out[s.strip + 1 : s.strip + 1 + s.field_halo, :] = aims[first_aim : first_aim + s.field_halo]


def optics_kernel(
    s, sides, weights, logits, aim, occupied, from_up, from_down, row_high, row_low, col_fwd, col_adj,
    adj_high, adj_low, features, shifted, terms,
    ext, aims, mask_high, mask_low, row_field, field, pulled_high, pulled_low, total,
    v_row_high, v_row_low, v_fwd, v_adj, v_adj_high, v_adj_low, v_features, sems,
):
    pairs = (
        (row_high, v_row_high), (row_low, v_row_low), (col_fwd, v_fwd), (col_adj, v_adj),
        (adj_high, v_adj_high), (adj_low, v_adj_low), (features, v_features),
    )
    copies = [pltpu.make_async_copy(a, b, sems.at[i]) for i, (a, b) in enumerate(pairs)]
    for copy in copies:
        copy.start()

    north = jnp.where(sides[2] > 0, from_up[...], 0.0)
    south = jnp.where(sides[3] > 0, from_down[...], 0.0)
    edge = up(s.strip, 8)
    lane_row = iota((edge, s.width), 0)
    ext[...] = jnp.zeros_like(ext)
    ext[s.base : s.base + s.grad_pad, :] = logits[...]
    ext[:edge, :] += jnp.where(lane_row < s.strip, north[:edge], 0.0)
    low = s.rows + s.base
    ext[low : low + edge, :] += jnp.where(lane_row < s.strip, south[:edge], 0.0)
    aims[...] = jnp.zeros_like(aims)
    aims[: s.field_halo, :] = north[s.strip + 1 : s.strip + 1 + s.field_halo]
    aims[s.field_halo : s.field_halo + s.rows, :] = aim[...]
    aims[s.field_halo + s.rows : s.field_rows, :] = south[s.strip + 1 : s.strip + 1 + s.field_halo]

    place = iota((s.depth, s.width), 0) - s.mask_halo
    used = jnp.where(place < 0, north[s.strip : s.strip + 1], 0.0)
    for r in range(s.rows // BLOCK):
        used = jnp.where((place >= r * BLOCK) & (place < (r + 1) * BLOCK), occupied[r : r + 1, :], used)
    below = (place >= s.rows) & (place < s.rows + s.mask_halo)
    used = jnp.where(below, south[s.strip : s.strip + 1], used)
    sigma = jax.nn.sigmoid(ext[...])
    mask = used * sigma
    mask_high[...], mask_low[...] = split(mask)
    slope = (mask * (1.0 - sigma))[s.base : s.base + s.grad_pad]
    slope = pltpu.roll(slope, s.width - s.base, 1)

    blocks = -(-s.field_cols // 128)
    total[...] = jnp.zeros_like(total)
    for copy in copies[:3]:
        copy.wait()

    def forward(f, carry):
        high, low = v_row_high[f], v_row_low[f]
        rowed = dot(high, mask_high[...]) + dot(high, mask_low[...]) + dot(low, mask_high[...])
        rowed_high, rowed_low = split(rowed)
        weight = weights[f // 2]
        for n in range(blocks):
            end = min(128 * n + 256, s.width)
            band = v_fwd[f][:, : end - 128 * n]
            both = dot(rowed_high[:, 128 * n : end], band, NT) + dot(rowed_low[:, 128 * n : end], band, NT)
            value = both[:, :128] + both[:, 128:]
            field[f, :, 128 * n : 128 * (n + 1)] = value
            total[:, 128 * n : 128 * (n + 1)] += weight * (value * value)
        return carry

    lax.fori_loop(0, s.filters, forward, 0)

    row, col = iota((s.field_pad, s.width), 0) - s.field_halo, iota((s.field_pad, s.width), 1) - s.field_halo
    inside = ((row >= 0) | (sides[2] > 0)) & ((row < s.rows) | (sides[3] > 0)) & (row < s.rows + s.field_halo)
    inside &= ((col >= 0) | (sides[0] > 0)) & ((col < s.cols) | (sides[1] > 0)) & (col < s.cols + s.field_halo)
    total[...] = jnp.where(inside, total[...] - aims[...], 0.0)
    copies[3].wait()
    out_blocks = -(-(s.cols + 2) // 128)
    if blocks * 128 < s.width:
        field[:, :, blocks * 128 :] = jnp.zeros_like(field[:, :, blocks * 128 :])

    def backward(f, carry):
        high, low = split(total[...] * field[f])
        start = pl.multiple_of(f * s.field_pad, 16)
        for n in range(out_blocks):
            end = min(128 * n + 256, s.width)
            band = v_adj[f][: end - 128 * n, :]
            both = dot(high[:, 128 * n : end], band) + dot(low[:, 128 * n : end], band)
            value = both[:, :128] + both[:, 128:]
            a, b = split(value)
            pulled_high[pl.ds(start, s.field_pad), 128 * n : 128 * (n + 1)] = a
            pulled_low[pl.ds(start, s.field_pad), 128 * n : 128 * (n + 1)] = b
        return carry

    lax.fori_loop(0, s.filters, backward, 0)
    if out_blocks * 128 < s.width:
        pulled_high[:, out_blocks * 128 :] = jnp.zeros_like(pulled_high[:, out_blocks * 128 :])
        pulled_low[:, out_blocks * 128 :] = jnp.zeros_like(pulled_low[:, out_blocks * 128 :])
    for copy in copies[4:6]:
        copy.wait()
    grad = dot(v_adj_high[...], pulled_high[...]) + dot(v_adj_high[...], pulled_low[...])
    grad = (grad + dot(v_adj_low[...], pulled_high[...])) * slope

    for b in range(3):
        moved = grad if b == 2 else pltpu.roll(grad, s.width - (2 - b), 1)
        shifted[b], shifted[3 + b] = split(moved[:, : s.cols])
    copies[6].wait()
    sums = jnp.zeros((s.channels * ROWS, 6 * WIN), F32)
    for k in range(s.steps):
        block = v_features[:, k * ROWS : (k + 1) * ROWS, :].reshape(s.channels * ROWS, s.cols)
        window = jnp.concatenate([shifted[q, k * ROWS : k * ROWS + WIN, :] for q in range(6)], 0)
        sums += dot(block, window, NT)
    cube = sums.reshape(s.channels, ROWS, 6 * WIN)
    u, lane = iota((ROWS, 6 * WIN), 0), iota((ROWS, 6 * WIN), 1)
    number, group = iota((16, 6 * WIN), 0), (iota((16, 6 * WIN), 1) // WIN) % 3
    result = jnp.zeros((16, s.channels), F32)
    for a in range(3):
        hit = jnp.where(lane % WIN == u - a + 2, 1.0, 0.0)
        line = (cube * hit[None]).sum(1)
        pick = jnp.where(number == a * 3 + group, 1.0, 0.0)
        result += dot(pick, line, NT, lax.Precision.HIGHEST)
    terms[...] = result


def feature_kernel(s, table, shifted, out):
    k = pl.program_id(0)
    start = pl.multiple_of(k * ROWS, ROWS)
    window = jnp.concatenate([shifted[q, pl.ds(start, WIN), :] for q in range(6)], 0)
    value = dot(table[:, : 6 * WIN], window)
    out[...] = value.astype(BF16).reshape(s.channels, ROWS, s.cols)


def spec(space=pltpu.VMEM):
    return pl.BlockSpec(memory_space=space)


def ring(value, axis, step):
    size = lax.axis_size(axis)
    return lax.ppermute(value, axis, [(i, (i + step) % size) for i in range(size)])


def summed(value, axis):
    size = lax.axis_size(axis)
    parts = [ring(value, axis, step) for step in range(1, size)]
    return functools.reduce(jnp.add, parts, value)


def on_device(features, conv_weight, row_taps, col_taps, kernel_weight, target, block_list):
    channels, tile_rows, tile_cols = features.shape
    s = Sizes(channels, tile_rows, tile_cols, row_taps.shape[2], row_taps.shape[0] * 2)
    shape = jax.ShapeDtypeStruct
    smem, hbm = spec(pltpu.SMEM), spec(pl.ANY)

    def call(body, outs, ins, scratch=(), limit=32):
        return pl.pallas_call(
            functools.partial(body, s),
            out_shape=outs,
            in_specs=ins,
            out_specs=jax.tree.map(lambda _: spec(), outs),
            scratch_shapes=list(scratch),
            compiler_params=pltpu.CompilerParams(vmem_limit_bytes=limit * MIB),
        )

    here_row, here_col = lax.axis_index("row"), lax.axis_index("col")
    sides = jnp.stack(
        [
            here_col > 0,
            here_col < lax.axis_size("col") - 1,
            here_row > 0,
            here_row < lax.axis_size("row") - 1,
        ]
    ).astype(jnp.int32)

    half_strip = shape((s.fold, 128), F32)
    table, partial, to_left, to_right = call(
        edge_kernel,
        (
            shape((channels * ROWS, 256), BF16),
            shape((s.grad_pad, s.width), F32),
            half_strip,
            half_strip,
        ),
        [smem, spec(), spec(), spec()],
        [pltpu.VMEM((3, s.rows + WIN, s.cols), F32)],
    )(block_list, features, conv_weight, target)
    from_right = ring(to_left, "col", -1)
    from_left = ring(to_right, "col", 1)

    filters = s.filters
    bands = call(
        band_kernel,
        (
            shape((filters, s.field_pad, s.depth), BF16),
            shape((filters, s.field_pad, s.depth), BF16),
            shape((filters, 256, 256), BF16),
            shape((filters, 256, 256), BF16),
            shape((s.grad_pad, filters * s.field_pad), BF16),
            shape((s.grad_pad, filters * s.field_pad), BF16),
        ),
        [spec(), spec(), smem],
        [pltpu.VMEM((filters * s.field_pad, s.depth), F32)],
    )(row_taps, col_taps, kernel_weight)

    row_strip = shape((s.strip_rows, s.width), F32)
    logits, aim, occupied, to_up, to_down = call(
        middle_kernel,
        (
            shape((s.grad_pad, s.width), F32),
            shape((s.rows, s.width), F32),
            shape((8, s.width), F32),
            row_strip,
            row_strip,
        ),
        [smem, smem, spec(), spec(), spec(), spec()],
    )(sides, block_list, partial, target, from_left, from_right)
    from_down = ring(to_up, "row", -1)
    from_up = ring(to_down, "row", 1)

    shifted, terms = call(
        optics_kernel,
        (shape((6, s.grad_pad, s.cols), BF16), shape((16, channels), F32)),
        [smem, smem] + [spec()] * 5 + [hbm] * 7,
        [
            pltpu.VMEM((s.depth, s.width), F32),
            pltpu.VMEM((s.field_pad, s.width), F32),
            pltpu.VMEM((s.depth, s.width), BF16),
            pltpu.VMEM((s.depth, s.width), BF16),
            pltpu.VMEM((8, 128), F32),
            pltpu.VMEM((filters, s.field_pad, s.width), F32),
            pltpu.VMEM((filters * s.field_pad, s.width), BF16),
            pltpu.VMEM((filters * s.field_pad, s.width), BF16),
            pltpu.VMEM((s.field_pad, s.width), F32),
        ]
        + [pltpu.VMEM(b.shape, BF16) for b in bands]
        + [pltpu.VMEM(features.shape, BF16), pltpu.SemaphoreType.DMA((7,))],
        48,
    )(sides, kernel_weight, logits, aim, occupied, from_up, from_down, *bands, features)

    by_row = summed(terms, "row")
    grad_features = pl.pallas_call(
        functools.partial(feature_kernel, s),
        out_shape=shape(features.shape, BF16),
        grid=(s.steps,),
        in_specs=[
            pl.BlockSpec((channels * ROWS, 256), lambda k: (0, 0)),
            pl.BlockSpec((6, s.grad_pad, s.cols), lambda k: (0, 0, 0)),
        ],
        out_specs=pl.BlockSpec((channels, ROWS, s.cols), lambda k: (0, k, 0)),
    )(table, shifted)
    whole = summed(by_row, "col")
    height = tile_rows * lax.axis_size("row")
    width = tile_cols * lax.axis_size("col")
    grad_weight = (whole[:9].T / math.sqrt(height * width)).reshape(channels, 3, 3)
    return (grad_weight, grad_features)


def solution(mesh):
    placed = (
        P(None, ("grp", "row"), "col"),
        P(),
        P(),
        P(),
        P(),
        P(("grp", "row"), "col"),
        P(("grp", "row"), "col", None),
    )
    return jax.shard_map(
        on_device,
        mesh=mesh,
        in_specs=placed,
        out_specs=(P("grp", None, None), P(None, ("grp", "row"), "col")),
        check_vma=False,
    )
```

```python
import functools
import math

import jax
import jax.numpy as jnp
from jax import lax
from jax.experimental import pallas as pl
from jax.experimental.pallas import tpu as pltpu
from jax.sharding import PartitionSpec as P

BLOCK = 64
ROWS = 16
WIN = 32
MIB = 1 << 20
F32 = jnp.float32
BF16 = jnp.bfloat16


def up(value, multiple):
    return -(-value // multiple) * multiple


def iota(shape, dim):
    return lax.broadcasted_iota(jnp.int32, shape, dim)


def split(value):
    high = value.astype(BF16)
    return high, (value - high.astype(F32)).astype(BF16)


def dot(left, right, dims=((1,), (0,)), precision=None):
    return lax.dot_general(
        left, right, (dims, ((), ())), precision=precision, preferred_element_type=F32
    )


NT = ((1,), (1,))


def neighbours(axis):
    here = lax.axis_index(axis)
    return here > 0, here < lax.axis_size(axis) - 1, here % 2 == 1


class Sizes:
    def __init__(self, channels, tile_rows, tile_cols, taps, filters):
        self.channels, self.rows, self.cols = channels, tile_rows, tile_cols
        self.taps, self.filters = taps, filters
        self.half = (taps - 1) // 2
        self.mask_halo = 2 * self.half + 1
        self.field_halo = self.half + 1
        self.strip = self.mask_halo + 1
        self.base = self.mask_halo - 1
        self.width = up(tile_cols + 2 * self.mask_halo, 128)
        self.field_rows = tile_rows + 2 * self.field_halo
        self.field_cols = tile_cols + 2 * self.field_halo
        self.field_pad = up(self.field_rows, 16)
        self.grad_pad = tile_rows + ROWS
        mask_rows = tile_rows + 2 * self.mask_halo
        self.depth = up(max(mask_rows, self.field_pad + taps), 128)
        self.steps = tile_rows // ROWS
        self.strip_rows = up(self.strip + 1 + self.field_halo, 8)
        self.fold = self.grad_pad // 2


def row_band_kernel(s, row_taps, kernel_weight, row_band, adj_high, adj_low, flipped):
    for f in range(s.filters):
        k, p = f // 2, f % 2
        pad = jnp.zeros((1, s.depth - s.taps), F32)
        row = jnp.concatenate([row_taps[k, p : p + 1, :], pad], 1)
        band = pltpu.roll(
            jnp.broadcast_to(row, (s.field_pad, s.depth)), 0, 1, stride=1, stride_axis=0
        )
        here = slice(f * s.field_pad, (f + 1) * s.field_pad)
        row_band[here, : s.depth], row_band[here, s.depth :] = split(band)
        flipped[here, :] = pltpu.roll(
            jnp.broadcast_to(row * (2.0 * kernel_weight[k]), (s.field_pad, s.depth)),
            s.depth - (s.taps - 1),
            1,
            stride=1,
            stride_axis=0,
        )
    turned = flipped[...].T[: s.grad_pad, :]
    adj_high[...], adj_low[...] = split(turned)


def col_band_kernel(s, col_taps, col_fwd, col_adj):
    for f in range(s.filters):
        k, p = f // 2, f % 2
        pad = jnp.zeros((1, 256 - s.taps), F32)
        wide = jnp.concatenate([col_taps[k, p : p + 1, :], pad], 1)
        band = pltpu.roll(jnp.broadcast_to(wide, (128, 256)), 0, 1, stride=1, stride_axis=0).T
        col_fwd[f, :, :128], col_fwd[f, :, 128:] = split(band)
        band = pltpu.roll(
            jnp.broadcast_to(wide, (256, 256)), 256 - (s.taps - 1), 1, stride=1, stride_axis=0
        )
        col_adj[f, :, :128], col_adj[f, :, 128:] = split(band[:, :128])


def edge_kernel(
    s, listed_hbm, features_hbm, conv_weight_hbm, target_hbm, table, partial, first_out, second_out,
    acc, listed, features, conv_weight, target, sems,
):
    fetch = [
        pltpu.make_async_copy(conv_weight_hbm, conv_weight, sems.at[0]),
        pltpu.make_async_copy(listed_hbm, listed, sems.at[1]),
        pltpu.make_async_copy(target_hbm, target, sems.at[2]),
    ]
    parts = 4
    rows = s.rows // parts
    for q in range(parts):
        here = pl.ds(q * rows, rows)
        fetch.append(
            pltpu.make_async_copy(features_hbm.at[:, here, :], features.at[:, here, :], sems.at[3 + q])
        )
    for copy in fetch:
        copy.start()
    acc[...] = jnp.zeros_like(acc)
    lanes = 3 * WIN
    u, lane = iota((s.channels * ROWS, lanes), 0) % ROWS, iota((s.channels * ROWS, lanes), 1)
    h = lane % WIN
    owner = jnp.where(
        iota((s.channels * ROWS, s.channels), 0) // ROWS == iota((s.channels * ROWS, s.channels), 1), 1.0, 0.0
    ).astype(BF16)
    pick = jnp.where(iota((3, lanes), 1) // WIN == iota((3, lanes), 0), 1.0, 0.0)
    fetch[0].wait()
    flat = jnp.zeros((s.channels * ROWS, lanes), F32)
    for row_shift in range(3):
        spread = dot(conv_weight[row_shift].astype(F32), pick, ((0,), (0,))).astype(BF16)
        flat = jnp.where(h == u - row_shift + 2, dot(owner, spread), flat)
    table[...] = jnp.concatenate([flat.astype(BF16)] * 3, 1)
    left = flat.T.astype(BF16)
    for k in range(s.steps):
        if k % (s.steps // parts) == 0:
            fetch[3 + k // (s.steps // parts)].wait()
        block = features[:, k * ROWS : (k + 1) * ROWS, :].reshape(s.channels * ROWS, s.cols)
        sums = dot(left, block)
        for b in range(3):
            acc[b, k * ROWS : k * ROWS + WIN, :] += sums[b * WIN : (b + 1) * WIN]
    fetch[1].wait()
    fetch[2].wait()
    whole = jnp.zeros((s.grad_pad, s.width), F32)
    blank = jnp.zeros((s.grad_pad, s.width - s.cols), F32)
    for b in range(3):
        part = jnp.concatenate([acc[b, : s.grad_pad], blank], 1)
        whole += pltpu.roll(part, s.base + 2 - b, 1)
    partial[...] = whole

    place, row = iota((s.grad_pad, 128), 1), iota((s.grad_pad, 128), 0)
    aim = jnp.concatenate([target[...], jnp.zeros((s.grad_pad - s.rows, s.cols), F32)], 0)
    aim = jnp.concatenate([aim, jnp.zeros((s.grad_pad, s.width - s.cols), F32)], 1)
    across = s.cols // BLOCK
    strips = []
    for first, first_aim, block_col in (
        (s.base, 0, 0),
        (s.cols, s.cols - s.field_halo, across - 1),
    ):
        logits = pltpu.roll(whole, (s.width - first) % s.width, 1)[:, :128]
        wanted = pltpu.roll(aim, (s.width - first_aim + s.strip) % s.width, 1)[:, :128]
        number = (row // BLOCK) * across + block_col
        used = jnp.zeros((s.grad_pad, 128), F32)
        for n in range(listed.shape[2]):
            used = jnp.where(number == listed[0, 0, n], 1.0, used)
        used = jnp.where(row < s.rows, used, 0.0)
        value = jnp.where(place < s.strip, logits, wanted)
        value = jnp.where(place < s.strip + s.field_halo, value, used)
        value = jnp.where(place < s.strip + s.field_halo + 1, value, 0.0)
        strips.append(
            jnp.where(iota((s.fold, 128), 1) < 64, value[: s.fold], pltpu.roll(value[s.fold :], 64, 1))
        )
    odd = neighbours("col")[2]
    first_out[...] = jnp.where(odd, strips[0], strips[1])
    second_out[...] = jnp.where(odd, strips[1], strips[0])


def unfolded(s, value):
    low = iota((s.fold, 128), 1) < 64
    return jnp.concatenate(
        [jnp.where(low, value, 0.0), jnp.where(low, pltpu.roll(value, 64, 1), 0.0)], 0
    )


def middle_kernel(s, listed, partial, target, first, second, band, logits, aim, occupied, first_out, second_out):
    extra = jnp.zeros((s.grad_pad, s.width - 128), F32)
    lane = iota((s.grad_pad, 128), 1)
    has_left, has_right, odd = neighbours("col")
    one, two = first[...], second[...]
    west = unfolded(s, jnp.where(has_left, jnp.where(odd, one, two), 0.0))
    east = unfolded(s, jnp.where(has_right, jnp.where(odd, two, one), 0.0))

    def placed(value, keep_from, keep, offset):
        kept = jnp.where((lane >= keep_from) & (lane < keep_from + keep), value, 0.0)
        wide = jnp.concatenate([kept, extra], 1)
        return pltpu.roll(wide, (offset - keep_from) % s.width, 1)

    whole = partial[...] + placed(west, 0, s.strip, 0)
    whole += placed(east, 0, s.strip, s.cols + s.base)
    logits[...] = whole
    own = jnp.concatenate([target[...], jnp.zeros((s.rows, s.width - s.cols), F32)], 1)
    aims = pltpu.roll(own, s.field_halo, 1)
    aims += placed(west, s.strip, s.field_halo, 0)[: s.rows]
    aims += placed(east, s.strip, s.field_halo, s.cols + s.field_halo)[: s.rows]
    aim[...] = aims

    across, down = s.cols // BLOCK, s.rows // BLOCK
    row, col = iota((8, s.width), 0), iota((8, s.width), 1) - s.mask_halo
    inside = (col >= 0) & (col < s.cols) & (row < down)
    number = jnp.where(inside, row * across + (col + BLOCK) // BLOCK - 1, -1)
    used = jnp.zeros((8, s.width), F32)
    for n in range(listed.shape[2]):
        used = jnp.where(number == listed[0, 0, n], 1.0, used)
    flag = s.strip + s.field_halo
    for r in range(down):
        here = row == r
        used = jnp.where(here & (col < 0), west[r * BLOCK : r * BLOCK + 1, flag : flag + 1], used)
        beyond = here & (col >= s.cols) & (col < s.cols + s.mask_halo)
        used = jnp.where(beyond, east[r * BLOCK : r * BLOCK + 1, flag : flag + 1], used)
    occupied[...] = used

    odd = neighbours("row")[2]

    def fill(out, low):
        start = s.rows + 2 - s.strip if low else 0
        start_aim = s.rows - s.field_halo if low else 0
        block_row = down - 1 if low else 0
        out[...] = jnp.zeros_like(out)
        out[: s.strip, :] = whole[start : start + s.strip]
        out[s.strip : s.strip + 1, :] = used[block_row : block_row + 1]
        out[s.strip + 1 : s.strip + 1 + s.field_halo, :] = aims[start_aim : start_aim + s.field_halo]

    @pl.when(odd)
    def _():
        fill(first_out, False)
        fill(second_out, True)

    @pl.when(jnp.logical_not(odd))
    def _():
        fill(first_out, True)
        fill(second_out, False)


def optics_kernel(
    s, weights, logits, aim, occupied, first, second, row_band, col_fwd, col_adj, adj_high, adj_low,
    features, shifted, terms,
    ext, aims, masks, field, pulled_high, pulled_low, total,
):

    has_left, has_right, _ = neighbours("col")
    has_up, has_down, odd = neighbours("row")
    one, two = first[...], second[...]
    north = jnp.where(has_up, jnp.where(odd, one, two), 0.0)
    south = jnp.where(has_down, jnp.where(odd, two, one), 0.0)
    edge = up(s.strip, 8)
    lane_row = iota((edge, s.width), 0)
    ext[...] = jnp.zeros_like(ext)
    ext[s.base : s.base + s.grad_pad, :] = logits[...]
    ext[:edge, :] += jnp.where(lane_row < s.strip, north[:edge], 0.0)
    low = s.rows + s.base
    ext[low : low + edge, :] += jnp.where(lane_row < s.strip, south[:edge], 0.0)
    aims[...] = jnp.zeros_like(aims)
    aims[: s.field_halo, :] = north[s.strip + 1 : s.strip + 1 + s.field_halo]
    aims[s.field_halo : s.field_halo + s.rows, :] = aim[...]
    aims[s.field_halo + s.rows : s.field_rows, :] = south[s.strip + 1 : s.strip + 1 + s.field_halo]

    place = iota((s.depth, s.width), 0) - s.mask_halo
    used = jnp.where(place < 0, north[s.strip : s.strip + 1], 0.0)
    for r in range(s.rows // BLOCK):
        used = jnp.where((place >= r * BLOCK) & (place < (r + 1) * BLOCK), occupied[r : r + 1, :], used)
    below = (place >= s.rows) & (place < s.rows + s.mask_halo)
    used = jnp.where(below, south[s.strip : s.strip + 1], used)
    sigma = jax.nn.sigmoid(ext[...])
    mask = used * sigma
    high, low = split(mask)
    masks[: s.depth, :] = high
    masks[s.depth : 2 * s.depth, :] = low
    masks[2 * s.depth :, :] = high
    slope = (mask * (1.0 - sigma))[s.base : s.base + s.grad_pad]
    slope = pltpu.roll(slope, s.width - s.base, 1)

    blocks = -(-s.field_cols // 128)
    total[...] = jnp.zeros_like(total)
    group = 4
    tall = group * s.field_pad
    gap = jnp.zeros((s.field_pad, 128), BF16)

    def windows(high, low, count):
        rows = []
        for n in range(count):
            line = []
            for part in (high, low):
                line.append(part[:, 128 * n : min(128 * n + 256, s.width)])
                if 128 * n + 256 > s.width:
                    line.append(gap)
            rows.append(jnp.concatenate(line, 1))
        return jnp.concatenate(rows, 0)

    def doubled(band):
        return jnp.concatenate([band, band], 0)

    def forward(g, carry):
        start = pl.multiple_of(g * tall, 16)
        band = row_band[pl.ds(start, tall), :]
        stack = jnp.concatenate([band[:, : s.depth], band[:, : s.depth], band[:, s.depth :]], 1)
        rowed = dot(stack, masks[...])
        for i in range(0, group, 2):
            squares = 0.0
            for f in (i, i + 1):
                high, low = split(rowed[f * s.field_pad : (f + 1) * s.field_pad])
                both = dot(windows(high, low, blocks), doubled(col_fwd[g * group + f]))
                value = both[:, :128] + both[:, 128:]
                for n in range(blocks):
                    here = slice(n * s.field_pad, (n + 1) * s.field_pad)
                    field[g * group + f, :, 128 * n : 128 * (n + 1)] = value[here]
                squares += value * value
            squares *= weights[(g * group + i) // 2]
            for n in range(blocks):
                total[:, 128 * n : 128 * (n + 1)] += squares[n * s.field_pad : (n + 1) * s.field_pad]
        return carry

    lax.fori_loop(0, s.filters // group, forward, 0)

    row, col = iota((s.field_pad, s.width), 0) - s.field_halo, iota((s.field_pad, s.width), 1) - s.field_halo
    inside = ((row >= 0) | has_up) & ((row < s.rows) | has_down) & (row < s.rows + s.field_halo)
    inside &= ((col >= 0) | has_left) & ((col < s.cols) | has_right) & (col < s.cols + s.field_halo)
    total[...] = jnp.where(inside, total[...] - aims[...], 0.0)
    out_blocks = -(-(s.cols + 2) // 128)
    if blocks * 128 < s.width:
        field[:, :, blocks * 128 :] = jnp.zeros_like(field[:, :, blocks * 128 :])

    def backward(g, carry):
        for i in range(group):
            f = g * group + i
            high, low = split(total[...] * field[f])
            start = pl.multiple_of(f * s.field_pad, 16)
            both = dot(windows(high, low, out_blocks), doubled(col_adj[f]))
            high, low = split(both[:, :128] + both[:, 128:])
            for n in range(out_blocks):
                here = slice(n * s.field_pad, (n + 1) * s.field_pad)
                pulled_high[pl.ds(start, s.field_pad), 128 * n : 128 * (n + 1)] = high[here]
                pulled_low[pl.ds(start, s.field_pad), 128 * n : 128 * (n + 1)] = low[here]
        return carry

    lax.fori_loop(0, s.filters // group, backward, 0)
    if out_blocks * 128 < s.width:
        pulled_high[:, out_blocks * 128 :] = jnp.zeros_like(pulled_high[:, out_blocks * 128 :])
        pulled_low[:, out_blocks * 128 :] = jnp.zeros_like(pulled_low[:, out_blocks * 128 :])
    both = dot(jnp.concatenate([adj_high[...], adj_low[...]], 0), pulled_high[...])
    grad = both[: s.grad_pad] + both[s.grad_pad :] + dot(adj_high[...], pulled_low[...])
    grad = grad * slope

    for b in range(3):
        moved = grad if b == 2 else pltpu.roll(grad, s.width - (2 - b), 1)
        moved = moved[:, : s.cols]
        shifted[b], shifted[3 + b] = split(moved)
        rest = moved - shifted[b].astype(F32) - shifted[3 + b].astype(F32)
        shifted[6 + b] = rest.astype(BF16)
    sums = jnp.zeros((s.channels * ROWS, 6 * WIN), F32)
    for k in range(s.steps):
        block = features[:, k * ROWS : (k + 1) * ROWS, :].reshape(s.channels * ROWS, s.cols)
        window = jnp.concatenate([shifted[q, k * ROWS : k * ROWS + WIN, :] for q in range(6)], 0)
        sums += dot(block, window, NT)
    cube = sums.reshape(s.channels, ROWS, 6 * WIN)
    u, lane = iota((ROWS, 6 * WIN), 0), iota((ROWS, 6 * WIN), 1)
    number, group = iota((16, 6 * WIN), 0), (iota((16, 6 * WIN), 1) // WIN) % 3
    result = jnp.zeros((16, s.channels), F32)
    for a in range(3):
        hit = jnp.where(lane % WIN == u - a + 2, 1.0, 0.0)
        line = (cube * hit[None]).sum(1)
        pick = jnp.where(number == a * 3 + group, 1.0, 0.0)
        result += dot(pick, line, NT, lax.Precision.HIGHEST)
    terms[...] = result


def feature_kernel(s, table, shifted, out, blocks, sems):
    copies = []
    for k in range(s.steps):
        window = jnp.concatenate([shifted[q, k * ROWS : k * ROWS + WIN, :] for q in range(9)], 0)
        value = dot(table[...], window)
        here = pl.ds(k * ROWS, ROWS)
        blocks[:, here, :] = value.astype(BF16).reshape(s.channels, ROWS, s.cols)
        copies.append(pltpu.make_async_copy(blocks.at[:, here, :], out.at[:, here, :], sems.at[k]))
        copies[-1].start()
    for copy in copies:
        copy.wait()


def spec(space=pltpu.VMEM):
    return pl.BlockSpec(memory_space=space)


def exchanged(first, second, axis):
    size, parts = lax.axis_size(axis), lax.axis_size("grp")
    one = lax.ppermute(first, axis, [(i, i ^ 1) for i in range(size)])
    pairs = []
    for g in range(parts):
        for i in range(size):
            j = i + 1 if i % 2 else i - 1
            if 0 <= j < size:
                pairs.append((g * size + i, g * size + j))
            elif parts % 2:
                pairs.append((g * size + i, g * size + (j % size)))
            else:
                pairs.append((g * size + i, (g ^ 1) * size + i))
    return one, lax.ppermute(second, ("grp", axis), pairs)


def summed(value, axis):
    size = lax.axis_size(axis)
    parts = [
        lax.ppermute(value, axis, [(i, i ^ step) for i in range(size)]) for step in range(1, size)
    ]
    return functools.reduce(jnp.add, parts, value)


def on_device(features, conv_weight, row_taps, col_taps, kernel_weight, target, block_list):
    channels, tile_rows, tile_cols = features.shape
    s = Sizes(channels, tile_rows, tile_cols, row_taps.shape[2], row_taps.shape[0] * 2)
    shape = jax.ShapeDtypeStruct
    smem, hbm = spec(pltpu.SMEM), spec(pltpu.HBM)

    def call(body, outs, ins, scratch=(), limit=24, out_space=pltpu.VMEM):
        return pl.pallas_call(
            functools.partial(body, s),
            out_shape=outs,
            in_specs=ins,
            out_specs=jax.tree.map(lambda _: spec(out_space), outs),
            scratch_shapes=list(scratch),
            compiler_params=pltpu.CompilerParams(vmem_limit_bytes=limit * MIB),
        )

    half_strip = shape((s.fold, 128), F32)
    table, partial, first, second = call(
        edge_kernel,
        (
            shape((channels * ROWS, 9 * WIN), BF16),
            shape((s.grad_pad, s.width), F32),
            half_strip,
            half_strip,
        ),
        [hbm] * 4,
        [
            pltpu.VMEM((3, s.rows + WIN, s.cols), F32),
            pltpu.SMEM(block_list.shape, jnp.int32),
            pltpu.VMEM(features.shape, BF16),
            pltpu.VMEM((3, 3, channels), BF16),
            pltpu.VMEM(target.shape, F32),
            pltpu.SemaphoreType.DMA((7,)),
        ],
    )(*(pltpu.with_memory_space_constraint(x, pltpu.HBM) for x in (block_list, features, conv_weight.transpose(1, 2, 0), target)))
    first, second = exchanged(first, second, "col")

    filters = s.filters
    col_bands = call(
        col_band_kernel,
        (shape((filters, 256, 256), BF16), shape((filters, 256, 256), BF16)),
        [spec()],
    )(col_taps)
    row_bands = call(
        row_band_kernel,
        (
            shape((filters * s.field_pad, 2 * s.depth), BF16),
            shape((s.grad_pad, filters * s.field_pad), BF16),
            shape((s.grad_pad, filters * s.field_pad), BF16),
        ),
        [spec(), smem],
        [pltpu.VMEM((filters * s.field_pad, s.depth), F32)],
    )(row_taps, kernel_weight)

    row_strip = shape((s.strip_rows, s.width), F32)
    logits, aim, occupied, first, second = call(
        middle_kernel,
        (
            shape((s.grad_pad, s.width), F32),
            shape((s.rows, s.width), F32),
            shape((8, s.width), F32),
            row_strip,
            row_strip,
        ),
        [smem, spec(), spec(), spec(), spec(), spec()],
    )(block_list, partial, target, first, second, col_bands[0])
    first, second = exchanged(first, second, "row")

    shifted, terms = call(
        optics_kernel,
        (shape((9, s.grad_pad, s.cols), BF16), shape((16, channels), F32)),
        [smem] + [spec()] * 11,
        [
            pltpu.VMEM((s.depth, s.width), F32),
            pltpu.VMEM((s.field_pad, s.width), F32),
            pltpu.VMEM((3 * s.depth, s.width), BF16),
            pltpu.VMEM((filters, s.field_pad, s.width), F32),
            pltpu.VMEM((filters * s.field_pad, s.width), BF16),
            pltpu.VMEM((filters * s.field_pad, s.width), BF16),
            pltpu.VMEM((s.field_pad, s.width), F32),
        ],
        32,
    )(kernel_weight, logits, aim, occupied, first, second, *row_bands[:1], *col_bands, *row_bands[1:], features)

    by_row = summed(terms, "row")
    grad_features = call(
        feature_kernel,
        shape(features.shape, BF16),
        [spec(), spec()],
        [pltpu.VMEM(features.shape, BF16), pltpu.SemaphoreType.DMA((s.steps,))],
        out_space=pltpu.HBM,
    )(table, shifted)
    whole = summed(by_row, "col")
    height = tile_rows * lax.axis_size("row")
    width = tile_cols * lax.axis_size("col")
    grad_weight = (whole[:9].T / math.sqrt(height * width)).reshape(channels, 3, 3)
    return (grad_weight, grad_features)


def solution(mesh):
    placed = (
        P(None, ("grp", "row"), "col"),
        P(),
        P(),
        P(),
        P(),
        P(("grp", "row"), "col"),
        P(("grp", "row"), "col", None),
    )
    return jax.shard_map(
        on_device,
        mesh=mesh,
        in_specs=placed,
        out_specs=(P("grp", None, None), P(None, ("grp", "row"), "col")),
        check_vma=False,
    )
```

```python
import functools
import math

import jax
import jax.numpy as jnp
from jax import lax
from jax.experimental import pallas as pl
from jax.experimental.pallas import tpu as pltpu
from jax.sharding import PartitionSpec as P

BLOCK = 64
ROWS = 16
WIN = 32
MIB = 1 << 20
F32 = jnp.float32
BF16 = jnp.bfloat16


def up(value, multiple):
    return -(-value // multiple) * multiple


def iota(shape, dim):
    return lax.broadcasted_iota(jnp.int32, shape, dim)


def split(value):
    high = value.astype(BF16)
    return high, (value - high.astype(F32)).astype(BF16)


def dot(left, right, dims=((1,), (0,)), precision=None):
    return lax.dot_general(
        left, right, (dims, ((), ())), precision=precision, preferred_element_type=F32
    )


NT = ((1,), (1,))


def neighbours(axis):
    here = lax.axis_index(axis)
    return here > 0, here < lax.axis_size(axis) - 1, here % 2 == 1


class Sizes:
    def __init__(self, channels, tile_rows, tile_cols, taps, filters):
        self.channels, self.rows, self.cols = channels, tile_rows, tile_cols
        self.taps, self.filters = taps, filters
        self.half = (taps - 1) // 2
        self.mask_halo = 2 * self.half + 1
        self.field_halo = self.half + 1
        self.strip = self.mask_halo + 1
        self.base = self.mask_halo - 1
        self.width = up(tile_cols + 2 * self.mask_halo, 128)
        self.field_rows = tile_rows + 2 * self.field_halo
        self.field_cols = tile_cols + 2 * self.field_halo
        self.field_pad = up(self.field_rows, 16)
        self.grad_pad = tile_rows + ROWS
        mask_rows = tile_rows + 2 * self.mask_halo
        self.depth = up(max(mask_rows, self.field_pad + taps), 128)
        self.steps = tile_rows // ROWS
        self.reach = taps - 1
        self.main = self.width - 128
        self.strip_rows = up(self.strip + 1 + self.field_halo, 8)
        self.fold = self.grad_pad // 2


def row_band_kernel(s, row_taps, weights, row_band, adj_high, adj_low, flipped):
    for f in range(s.filters):
        k, p = f // 2, f % 2
        pad = jnp.zeros((1, s.depth - s.taps), F32)
        row = jnp.concatenate([row_taps[k, p : p + 1, :], pad], 1)
        band = pltpu.roll(
            jnp.broadcast_to(row, (s.field_pad, s.depth)), 0, 1, stride=1, stride_axis=0
        )
        here = slice(f * s.field_pad, (f + 1) * s.field_pad)
        row_band[here, : s.depth], row_band[here, s.depth :] = split(band)
        flipped[here, :] = pltpu.roll(
            jnp.broadcast_to(row * (2.0 * weights[k : k + 1, :1]), (s.field_pad, s.depth)),
            s.depth - s.reach,
            1,
            stride=1,
            stride_axis=0,
        )
    turned = flipped[...].T[: s.grad_pad, :]
    adj_high[...], adj_low[...] = split(turned)


def col_band_kernel(s, col_taps, fwd_main, fwd_last, adj_main, adj_last):
    early = iota((128, 128), 1) < 128 - s.reach
    blocks = s.main // 128
    blank = jnp.zeros((128, 128), BF16)

    def fill(out, f, same, below):
        ends = split(jnp.where(early, same, 0.0))
        same, below = split(same), split(below)
        for part in range(2):
            for i in range(blocks):
                for j in range(blocks):
                    piece = blank
                    if i == j:
                        piece = ends[part] if j == blocks - 1 else same[part]
                    elif i == j + 1:
                        piece = below[part]
                    out[f, part, 128 * i : 128 * (i + 1), 128 * j : 128 * (j + 1)] = piece

    for f in range(s.filters):
        k, p = f // 2, f % 2
        pad = jnp.zeros((1, 256 - s.taps), F32)
        wide = jnp.concatenate([col_taps[k, p : p + 1, :], pad], 1)
        band = pltpu.roll(jnp.broadcast_to(wide, (128, 256)), 0, 1, stride=1, stride_axis=0)
        turned = band.T
        fill(fwd_main, f, turned[:128], turned[128:])
        corner = jnp.concatenate([band[: 128 - s.reach, :128], band[: s.reach, :128]], 0).T
        fwd_last[f, :, :128], fwd_last[f, :, 128:] = split(corner)
        band = pltpu.roll(
            jnp.broadcast_to(wide, (256, 256)), 256 - s.reach, 1, stride=1, stride_axis=0
        )[:, :128]
        fill(adj_main, f, band[:128], band[128:])
        corner = pltpu.roll(
            jnp.broadcast_to(wide[:, :128], (128, 128)), 128 - 2 * s.reach, 1, stride=1, stride_axis=0
        )
        adj_last[f, :, :128], adj_last[f, :, 128:] = split(corner)


def edge_kernel(
    s, listed_hbm, features_hbm, conv_weight_hbm, target_hbm, row_taps_hbm, col_taps_hbm, weights_hbm,
    table, partial, first_out, second_out, features, target, row_taps, col_taps, weights_out, own,
    acc, listed, conv_weight, weights, sems,
):
    fetch = [
        pltpu.make_async_copy(conv_weight_hbm, conv_weight, sems.at[0]),
        pltpu.make_async_copy(listed_hbm, listed, sems.at[1]),
        pltpu.make_async_copy(target_hbm, target, sems.at[2]),
        pltpu.make_async_copy(row_taps_hbm, row_taps, sems.at[7]),
        pltpu.make_async_copy(col_taps_hbm, col_taps, sems.at[8]),
        pltpu.make_async_copy(weights_hbm, weights, sems.at[9]),
    ]
    slow = len(fetch)
    parts = 4
    rows = s.rows // parts
    for q in range(parts):
        here = pl.ds(q * rows, rows)
        fetch.append(
            pltpu.make_async_copy(features_hbm.at[:, here, :], features.at[:, here, :], sems.at[3 + q])
        )
    for copy in fetch:
        copy.start()
    acc[...] = jnp.zeros_like(acc)
    lanes = 3 * WIN
    u, lane = iota((s.channels * ROWS, lanes), 0) % ROWS, iota((s.channels * ROWS, lanes), 1)
    h = lane % WIN
    owner = jnp.where(
        iota((s.channels * ROWS, s.channels), 0) // ROWS == iota((s.channels * ROWS, s.channels), 1), 1.0, 0.0
    ).astype(BF16)
    pick = jnp.where(iota((3, lanes), 1) // WIN == iota((3, lanes), 0), 1.0, 0.0)
    fetch[0].wait()
    flat = jnp.zeros((s.channels * ROWS, lanes), F32)
    for row_shift in range(3):
        spread = dot(conv_weight[row_shift].astype(F32), pick, ((0,), (0,))).astype(BF16)
        flat = jnp.where(h == u - row_shift + 2, dot(owner, spread), flat)
    table[...] = jnp.concatenate([flat.astype(BF16)] * 3, 1)
    left = flat.T.astype(BF16)
    for k in range(s.steps):
        if k % (s.steps // parts) == 0:
            fetch[slow + k // (s.steps // parts)].wait()
        block = features[:, k * ROWS : (k + 1) * ROWS, :].reshape(s.channels * ROWS, s.cols)
        sums = dot(left, block)
        for b in range(3):
            acc[b, k * ROWS : k * ROWS + WIN, :] += sums[b * WIN : (b + 1) * WIN]
    for copy in fetch[1:slow]:
        copy.wait()
    for k in range(s.filters // 2):
        weights_out[k : k + 1, :] = jnp.broadcast_to(weights[k], (1, 128))
    across, down = s.cols // BLOCK, s.rows // BLOCK
    row, col = iota((8, s.width), 0), iota((8, s.width), 1) - s.mask_halo
    inside = (col >= 0) & (col < s.cols) & (row < down)
    number = jnp.where(inside, row * across + (col + BLOCK) // BLOCK - 1, -1)
    used = jnp.zeros((8, s.width), F32)
    for n in range(listed.shape[2]):
        used = jnp.where(number == listed[0, 0, n], 1.0, used)
    own[...] = used
    whole = jnp.zeros((s.grad_pad, s.width), F32)
    blank = jnp.zeros((s.grad_pad, s.width - s.cols), F32)
    for b in range(3):
        part = jnp.concatenate([acc[b, : s.grad_pad], blank], 1)
        whole += pltpu.roll(part, s.base + 2 - b, 1)
    partial[...] = whole

    place, row = iota((s.grad_pad, 128), 1), iota((s.grad_pad, 128), 0)
    aim = jnp.concatenate([target[...], jnp.zeros((s.grad_pad - s.rows, s.cols), F32)], 0)
    aim = jnp.concatenate([aim, jnp.zeros((s.grad_pad, s.width - s.cols), F32)], 1)
    strips = []
    for first, first_aim, block_col in (
        (s.base, 0, 0),
        (s.cols, s.cols - s.field_halo, across - 1),
    ):
        logits = pltpu.roll(whole, (s.width - first) % s.width, 1)[:, :128]
        wanted = pltpu.roll(aim, (s.width - first_aim + s.strip) % s.width, 1)[:, :128]
        number = (row // BLOCK) * across + block_col
        used = jnp.zeros((s.grad_pad, 128), F32)
        for n in range(listed.shape[2]):
            used = jnp.where(number == listed[0, 0, n], 1.0, used)
        used = jnp.where(row < s.rows, used, 0.0)
        value = jnp.where(place < s.strip, logits, wanted)
        value = jnp.where(place < s.strip + s.field_halo, value, used)
        value = jnp.where(place < s.strip + s.field_halo + 1, value, 0.0)
        strips.append(
            jnp.where(iota((s.fold, 128), 1) < 64, value[: s.fold], pltpu.roll(value[s.fold :], 64, 1))
        )
    odd = neighbours("col")[2]
    first_out[...] = jnp.where(odd, strips[0], strips[1])
    second_out[...] = jnp.where(odd, strips[1], strips[0])


def unfolded(s, value):
    low = iota((s.fold, 128), 1) < 64
    return jnp.concatenate(
        [jnp.where(low, value, 0.0), jnp.where(low, pltpu.roll(value, 64, 1), 0.0)], 0
    )


def middle_kernel(s, own_used, partial, target, first, second, band, logits, aim, occupied, first_out, second_out):
    extra = jnp.zeros((s.grad_pad, s.width - 128), F32)
    lane = iota((s.grad_pad, 128), 1)
    has_left, has_right, odd = neighbours("col")
    one, two = first[...], second[...]
    west = unfolded(s, jnp.where(has_left, jnp.where(odd, one, two), 0.0))
    east = unfolded(s, jnp.where(has_right, jnp.where(odd, two, one), 0.0))

    def placed(value, keep_from, keep, offset):
        kept = jnp.where((lane >= keep_from) & (lane < keep_from + keep), value, 0.0)
        wide = jnp.concatenate([kept, extra], 1)
        return pltpu.roll(wide, (offset - keep_from) % s.width, 1)

    whole = partial[...] + placed(west, 0, s.strip, 0)
    whole += placed(east, 0, s.strip, s.cols + s.base)
    logits[...] = whole
    own = jnp.concatenate([target[...], jnp.zeros((s.rows, s.width - s.cols), F32)], 1)
    aims = pltpu.roll(own, s.field_halo, 1)
    aims += placed(west, s.strip, s.field_halo, 0)[: s.rows]
    aims += placed(east, s.strip, s.field_halo, s.cols + s.field_halo)[: s.rows]
    aim[...] = aims

    down = s.rows // BLOCK
    row, col = iota((8, s.width), 0), iota((8, s.width), 1) - s.mask_halo
    used = own_used[...]
    flag = s.strip + s.field_halo
    for r in range(down):
        here = row == r
        used = jnp.where(here & (col < 0), west[r * BLOCK : r * BLOCK + 1, flag : flag + 1], used)
        beyond = here & (col >= s.cols) & (col < s.cols + s.mask_halo)
        used = jnp.where(beyond, east[r * BLOCK : r * BLOCK + 1, flag : flag + 1], used)
    occupied[...] = used

    odd = neighbours("row")[2]

    def fill(out, low):
        start = s.rows + 2 - s.strip if low else 0
        start_aim = s.rows - s.field_halo if low else 0
        block_row = down - 1 if low else 0
        out[...] = jnp.zeros_like(out)
        out[: s.strip, :] = whole[start : start + s.strip]
        out[s.strip : s.strip + 1, :] = used[block_row : block_row + 1]
        out[s.strip + 1 : s.strip + 1 + s.field_halo, :] = aims[start_aim : start_aim + s.field_halo]

    @pl.when(odd)
    def _():
        fill(first_out, False)
        fill(second_out, True)

    @pl.when(jnp.logical_not(odd))
    def _():
        fill(first_out, True)
        fill(second_out, False)


def overlapped(s, value):
    return jnp.concatenate([value[:, : s.main], pltpu.roll(value, s.reach, 1)[:, s.main :]], 1)


def optics_kernel(
    s, weights, logits, aim, occupied, first, second, row_band, fwd_main, fwd_last, adj_main, adj_last, adj_high, adj_low,
    features, shifted, terms,
    ext, aims, masks, field, pulled, total,
):

    has_left, has_right, _ = neighbours("col")
    has_up, has_down, odd = neighbours("row")
    one, two = first[...], second[...]
    north = jnp.where(has_up, jnp.where(odd, one, two), 0.0)
    south = jnp.where(has_down, jnp.where(odd, two, one), 0.0)
    edge = up(s.strip, 8)
    lane_row = iota((edge, s.width), 0)
    ext[...] = jnp.zeros_like(ext)
    ext[s.base : s.base + s.grad_pad, :] = logits[...]
    ext[:edge, :] += jnp.where(lane_row < s.strip, north[:edge], 0.0)
    low = s.rows + s.base
    ext[low : low + edge, :] += jnp.where(lane_row < s.strip, south[:edge], 0.0)
    aims[...] = jnp.zeros_like(aims)
    aims[: s.field_halo, :] = north[s.strip + 1 : s.strip + 1 + s.field_halo]
    aims[s.field_halo : s.field_halo + s.rows, :] = aim[...]
    aims[s.field_halo + s.rows : s.field_rows, :] = south[s.strip + 1 : s.strip + 1 + s.field_halo]

    place = iota((s.depth, s.width), 0) - s.mask_halo
    used = jnp.where(place < 0, north[s.strip : s.strip + 1], 0.0)
    for r in range(s.rows // BLOCK):
        used = jnp.where((place >= r * BLOCK) & (place < (r + 1) * BLOCK), occupied[r : r + 1, :], used)
    below = (place >= s.rows) & (place < s.rows + s.mask_halo)
    used = jnp.where(below, south[s.strip : s.strip + 1], used)
    sigma = jax.nn.sigmoid(ext[...])
    mask = used * sigma
    high, low = split(overlapped(s, mask))
    for here in (slice(0, s.depth), slice(s.depth, 2 * s.depth)):
        masks[here, : s.width] = high
        masks[here, s.width :] = low
    slope = (mask * (1.0 - sigma))[s.base : s.base + s.grad_pad]
    slope = pltpu.roll(slope, s.width - s.base, 1)

    total[...] = jnp.zeros_like(total)
    group = 4
    tall = group * s.field_pad
    late = iota((s.field_pad, 128), 1) >= 128 - s.reach

    def banded(high, low, main, last):
        ends = jnp.concatenate([high[:, s.main :], low[:, s.main :]], 1)
        both = dot(ends, jnp.concatenate([last, last], 0))
        tail = both[:, :128] + both[:, 128:]
        high, low = high[:, : s.main], low[:, : s.main]
        stack = jnp.concatenate([main[0], main[0], main[1]], 0)
        head = dot(jnp.concatenate([high, low, high], 1), stack)
        seam = head[:, s.main - 128 :] + jnp.where(late, tail, 0.0)
        pieces = [seam, tail]
        if s.main > 128:
            pieces.insert(0, head[:, : s.main - 128])
        return jnp.concatenate(pieces, 1)

    for g in range(s.filters // group):
        band = row_band[g * tall : (g + 1) * tall, :]
        one = dot(band, masks[:, : s.width + 128])
        two = dot(band[:, : s.depth], masks[: s.depth, s.width + 128 :])
        rowed = one[:, : s.width] + jnp.concatenate([one[:, s.width :], two], 1)
        for i in range(0, group, 2):
            squares = 0.0
            for j in (i, i + 1):
                f = g * group + j
                high, low = split(rowed[j * s.field_pad : (j + 1) * s.field_pad])
                value = banded(high, low, fwd_main[f], fwd_last[f])
                field[f] = value
                squares += value * value
            k = (g * group + i) // 2
            total[...] += squares * weights[k : k + 1, :1]

    row, lane = iota((s.field_pad, s.width), 0) - s.field_halo, iota((s.field_pad, s.width), 1)
    col = jnp.where(lane < s.main, lane, lane - s.reach) - s.field_halo
    inside = ((row >= 0) | has_up) & ((row < s.rows) | has_down) & (row < s.rows + s.field_halo)
    inside &= ((col >= 0) | has_left) & ((col < s.cols) | has_right) & (col < s.cols + s.field_halo)
    total[...] = jnp.where(inside, total[...] - overlapped(s, aims[...]), 0.0)

    for f in range(s.filters):
        high, low = split(total[...] * field[f])
        high, low = split(banded(high, low, adj_main[f], adj_last[f]))
        rows = slice(f * s.field_pad, (f + 1) * s.field_pad)
        pulled[rows, : s.width] = high
        pulled[rows, s.width : s.width + 128] = low[:, s.main :]
        pulled[rows, s.width + 128 :] = low[:, : s.main]

    both = dot(jnp.concatenate([adj_high[...], adj_low[...]], 0), pulled[:, : s.width + 128])
    rest = both[: s.grad_pad, s.width :]
    both = both[: s.grad_pad, : s.width] + both[s.grad_pad :, : s.width]
    low = dot(adj_high[...], pulled[:, s.width + 128 :])
    grad = jnp.concatenate([both[:, : s.main] + low, both[:, s.main :] + rest], 1) * slope

    for b in range(3):
        moved = grad if b == 2 else pltpu.roll(grad, s.width - (2 - b), 1)
        moved = moved[:, : s.cols]
        shifted[b], shifted[3 + b] = split(moved)
        rest = moved - shifted[b].astype(F32) - shifted[3 + b].astype(F32)
        shifted[6 + b] = rest.astype(BF16)
    sums = jnp.zeros((s.channels * ROWS, 6 * WIN), F32)
    for k in range(s.steps):
        block = features[:, k * ROWS : (k + 1) * ROWS, :].reshape(s.channels * ROWS, s.cols)
        window = jnp.concatenate([shifted[q, k * ROWS : k * ROWS + WIN, :] for q in range(6)], 0)
        sums += dot(block, window, NT)
    cube = sums.reshape(s.channels, ROWS, 6 * WIN)
    u, lane = iota((ROWS, 6 * WIN), 0), iota((ROWS, 6 * WIN), 1)
    number, group = iota((16, 6 * WIN), 0), (iota((16, 6 * WIN), 1) // WIN) % 3
    result = jnp.zeros((16, s.channels), F32)
    for a in range(3):
        hit = jnp.where(lane % WIN == u - a + 2, 1.0, 0.0)
        line = (cube * hit[None]).sum(1)
        pick = jnp.where(number == a * 3 + group, 1.0, 0.0)
        result += dot(pick, line, NT, lax.Precision.HIGHEST)
    terms[...] = result


def feature_kernel(s, table, shifted, out, blocks, sems):
    copies = []
    for k in range(s.steps):
        window = jnp.concatenate([shifted[q, k * ROWS : k * ROWS + WIN, :] for q in range(9)], 0)
        value = dot(table[...], window)
        here = pl.ds(k * ROWS, ROWS)
        blocks[:, here, :] = value.astype(BF16).reshape(s.channels, ROWS, s.cols)
        copies.append(pltpu.make_async_copy(blocks.at[:, here, :], out.at[:, here, :], sems.at[k]))
        copies[-1].start()
    for copy in copies:
        copy.wait()


def spec(space=pltpu.VMEM):
    return pl.BlockSpec(memory_space=space)


def exchanged(first, second, axis):
    size, parts = lax.axis_size(axis), lax.axis_size("grp")
    one = lax.ppermute(first, axis, [(i, i ^ 1) for i in range(size)])
    pairs = []
    for g in range(parts):
        for i in range(size):
            j = i + 1 if i % 2 else i - 1
            if 0 <= j < size:
                pairs.append((g * size + i, g * size + j))
            elif parts % 2:
                pairs.append((g * size + i, g * size + (j % size)))
            else:
                pairs.append((g * size + i, (g ^ 1) * size + i))
    return one, lax.ppermute(second, ("grp", axis), pairs)


def summed(value, axis):
    size = lax.axis_size(axis)
    parts = [
        lax.ppermute(value, axis, [(i, i ^ step) for i in range(size)]) for step in range(1, size)
    ]
    return functools.reduce(jnp.add, parts, value)


def on_device(features, conv_weight, row_taps, col_taps, kernel_weight, target, block_list):
    channels, tile_rows, tile_cols = features.shape
    s = Sizes(channels, tile_rows, tile_cols, row_taps.shape[2], row_taps.shape[0] * 2)
    shape = jax.ShapeDtypeStruct
    hbm = spec(pltpu.HBM)

    def call(body, outs, ins, scratch=(), limit=24, out_space=pltpu.VMEM):
        return pl.pallas_call(
            functools.partial(body, s),
            out_shape=outs,
            in_specs=ins,
            out_specs=jax.tree.map(lambda _: spec(out_space), outs),
            scratch_shapes=list(scratch),
            compiler_params=pltpu.CompilerParams(vmem_limit_bytes=limit * MIB),
        )

    half_strip = shape((s.fold, 128), F32)
    table, partial, first, second, features_here, target_here, row_here, col_here, weights, own = call(
        edge_kernel,
        (
            shape((channels * ROWS, 9 * WIN), BF16),
            shape((s.grad_pad, s.width), F32),
            half_strip,
            half_strip,
            shape(features.shape, BF16),
            shape(target.shape, F32),
            shape(row_taps.shape, F32),
            shape(col_taps.shape, F32),
            shape((8 * -(-s.filters // 16), 128), F32),
            shape((8, s.width), F32),
        ),
        [hbm] * 7,
        [
            pltpu.VMEM((3, s.rows + WIN, s.cols), F32),
            pltpu.SMEM(block_list.shape, jnp.int32),
            pltpu.VMEM((3, 3, channels), BF16),
            pltpu.SMEM(kernel_weight.shape, F32),
            pltpu.SemaphoreType.DMA((10,)),
        ],
    )(
        *(
            pltpu.with_memory_space_constraint(x, pltpu.HBM)
            for x in (
                block_list, features, conv_weight.transpose(1, 2, 0), target, row_taps, col_taps,
                kernel_weight,
            )
        )
    )
    first, second = exchanged(first, second, "col")

    filters = s.filters
    col_bands = call(
        col_band_kernel,
        (shape((filters, 2, s.main, s.main), BF16), shape((filters, 128, 256), BF16)) * 2,
        [spec()],
    )(col_here)
    row_bands = call(
        row_band_kernel,
        (
            shape((filters * s.field_pad, 2 * s.depth), BF16),
            shape((s.grad_pad, filters * s.field_pad), BF16),
            shape((s.grad_pad, filters * s.field_pad), BF16),
        ),
        [spec(), spec()],
        [pltpu.VMEM((filters * s.field_pad, s.depth), F32)],
    )(row_here, weights)

    row_strip = shape((s.strip_rows, s.width), F32)
    logits, aim, occupied, first, second = call(
        middle_kernel,
        (
            shape((s.grad_pad, s.width), F32),
            shape((s.rows, s.width), F32),
            shape((8, s.width), F32),
            row_strip,
            row_strip,
        ),
        [spec()] * 6,
    )(own, partial, target_here, first, second, col_bands[1])
    first, second = exchanged(first, second, "row")

    shifted, terms = call(
        optics_kernel,
        (shape((9, s.grad_pad, s.cols), BF16), shape((16, channels), F32)),
        [spec()] * 14,
        [
            pltpu.VMEM((s.depth, s.width), F32),
            pltpu.VMEM((s.field_pad, s.width), F32),
            pltpu.VMEM((2 * s.depth, 2 * s.width), BF16),
            pltpu.VMEM((filters, s.field_pad, s.width), F32),
            pltpu.VMEM((filters * s.field_pad, 2 * s.width), BF16),
            pltpu.VMEM((s.field_pad, s.width), F32),
        ],
        32,
    )(weights, logits, aim, occupied, first, second, *row_bands[:1], *col_bands, *row_bands[1:], features_here)

    by_row = summed(terms, "row")
    grad_features = call(
        feature_kernel,
        shape(features.shape, BF16),
        [spec(), spec()],
        [pltpu.VMEM(features.shape, BF16), pltpu.SemaphoreType.DMA((s.steps,))],
        out_space=pltpu.HBM,
    )(table, shifted)
    whole = summed(by_row, "col")
    height = tile_rows * lax.axis_size("row")
    width = tile_cols * lax.axis_size("col")
    grad_weight = (whole[:9].T / math.sqrt(height * width)).reshape(channels, 3, 3)
    return (grad_weight, grad_features)


def solution(mesh):
    placed = (
        P(None, ("grp", "row"), "col"),
        P(),
        P(),
        P(),
        P(),
        P(("grp", "row"), "col"),
        P(("grp", "row"), "col", None),
    )
    return jax.shard_map(
        on_device,
        mesh=mesh,
        in_specs=placed,
        out_specs=(P("grp", None, None), P(None, ("grp", "row"), "col")),
        check_vma=False,
    )
```

```python
import functools
import math

import jax
import jax.numpy as jnp
from jax import lax
from jax.experimental import pallas as pl
from jax.experimental.pallas import tpu as pltpu
from jax.sharding import PartitionSpec as P

BLOCK = 64
ROWS = 16
WIN = 32
MIB = 1 << 20
F32 = jnp.float32
BF16 = jnp.bfloat16


def up(value, multiple):
    return -(-value // multiple) * multiple


def iota(shape, dim):
    return lax.broadcasted_iota(jnp.int32, shape, dim)


def split(value):
    high = value.astype(BF16)
    return high, (value - high.astype(F32)).astype(BF16)


def dot(left, right, dims=((1,), (0,)), precision=None):
    return lax.dot_general(
        left, right, (dims, ((), ())), precision=precision, preferred_element_type=F32
    )


NT = ((1,), (1,))


def neighbours(axis):
    here = lax.axis_index(axis)
    return here > 0, here < lax.axis_size(axis) - 1, here % 2 == 1


class Sizes:
    def __init__(self, channels, tile_rows, tile_cols, taps, filters):
        self.channels, self.rows, self.cols = channels, tile_rows, tile_cols
        self.taps, self.filters = taps, filters
        self.half = (taps - 1) // 2
        self.mask_halo = 2 * self.half + 1
        self.field_halo = self.half + 1
        self.strip = self.mask_halo + 1
        self.base = self.mask_halo - 1
        self.width = up(tile_cols + 2 * self.mask_halo, 128)
        self.field_rows = tile_rows + 2 * self.field_halo
        self.field_cols = tile_cols + 2 * self.field_halo
        self.field_pad = up(self.field_rows, 16)
        self.grad_pad = tile_rows + ROWS
        mask_rows = tile_rows + 2 * self.mask_halo
        self.mask_pad = up(mask_rows, 16)
        self.depth = up(max(mask_rows, self.field_pad + taps), 128)
        self.steps = tile_rows // ROWS
        self.reach = taps - 1
        self.main = self.width - 128
        self.strip_rows = up(self.strip + 1 + self.field_halo, 8)
        self.fold = self.grad_pad // 2


def row_band_kernel(s, row_taps, weights, row_band, adj_high, adj_low, flipped):
    for f in range(s.filters):
        k, p = f // 2, f % 2
        pad = jnp.zeros((1, s.depth - s.taps), F32)
        row = jnp.concatenate([row_taps[k, p : p + 1, :], pad], 1)
        band = pltpu.roll(
            jnp.broadcast_to(row, (s.field_pad, s.depth)), 0, 1, stride=1, stride_axis=0
        )
        here = slice(f * s.field_pad, (f + 1) * s.field_pad)
        row_band[here, : s.depth], row_band[here, s.depth :] = split(band)
        flipped[here, :] = pltpu.roll(
            jnp.broadcast_to(row * (2.0 * weights[k : k + 1, :1]), (s.field_pad, s.depth)),
            s.depth - s.reach,
            1,
            stride=1,
            stride_axis=0,
        )
    turned = flipped[...].T[: s.grad_pad, :]
    adj_high[...], adj_low[...] = split(turned)


def col_band_kernel(s, col_taps, fwd_main, fwd_last, adj_main, adj_last):
    early = iota((128, 128), 1) < 128 - s.reach
    blocks = s.main // 128
    blank = jnp.zeros((128, 128), BF16)

    def fill(out, f, same, below):
        ends = split(jnp.where(early, same, 0.0))
        same, below = split(same), split(below)
        for part in range(2):
            for i in range(blocks):
                for j in range(blocks):
                    piece = blank
                    if i == j:
                        piece = ends[part] if j == blocks - 1 else same[part]
                    elif i == j + 1:
                        piece = below[part]
                    out[f, part, 128 * i : 128 * (i + 1), 128 * j : 128 * (j + 1)] = piece

    for f in range(s.filters):
        k, p = f // 2, f % 2
        pad = jnp.zeros((1, 256 - s.taps), F32)
        wide = jnp.concatenate([col_taps[k, p : p + 1, :], pad], 1)
        band = pltpu.roll(jnp.broadcast_to(wide, (128, 256)), 0, 1, stride=1, stride_axis=0)
        turned = band.T
        fill(fwd_main, f, turned[:128], turned[128:])
        corner = jnp.concatenate([band[: 128 - s.reach, :128], band[: s.reach, :128]], 0).T
        fwd_last[f, :, :128], fwd_last[f, :, 128:] = split(corner)
        band = pltpu.roll(
            jnp.broadcast_to(wide, (256, 256)), 256 - s.reach, 1, stride=1, stride_axis=0
        )[:, :128]
        fill(adj_main, f, band[:128], band[128:])
        corner = pltpu.roll(
            jnp.broadcast_to(wide[:, :128], (128, 128)), 128 - 2 * s.reach, 1, stride=1, stride_axis=0
        )
        adj_last[f, :, :128], adj_last[f, :, 128:] = split(corner)


def pulled_tile(value, start, lane):
    first = start // 128 * 128
    tile = value[:, first : first + 128]
    shift = (lane - start) % 128
    return pltpu.roll(tile, shift, 1) if shift else tile


def edge_kernel(
    s, listed_hbm, features_hbm, conv_weight_hbm, target_hbm, row_taps_hbm, col_taps_hbm, weights_hbm,
    table, partial, first_out, second_out, features, target, row_taps, col_taps, weights_out, own,
    acc, listed, conv_weight, weights, sems,
):
    fetch = [
        pltpu.make_async_copy(conv_weight_hbm, conv_weight, sems.at[0]),
        pltpu.make_async_copy(listed_hbm, listed, sems.at[1]),
        pltpu.make_async_copy(target_hbm, target, sems.at[2]),
        pltpu.make_async_copy(row_taps_hbm, row_taps, sems.at[7]),
        pltpu.make_async_copy(col_taps_hbm, col_taps, sems.at[8]),
        pltpu.make_async_copy(weights_hbm, weights, sems.at[9]),
    ]
    slow = len(fetch)
    parts = 4
    rows = s.rows // parts
    for q in range(parts):
        here = pl.ds(q * rows, rows)
        fetch.append(
            pltpu.make_async_copy(features_hbm.at[:, here, :], features.at[:, here, :], sems.at[3 + q])
        )
    for copy in fetch:
        copy.start()
    acc[...] = jnp.zeros_like(acc)
    lanes = 128
    u, lane = iota((s.channels * ROWS, lanes), 0) % ROWS, iota((s.channels * ROWS, lanes), 1)
    h = lane % WIN
    owner = jnp.where(
        iota((s.channels * ROWS, s.channels), 0) // ROWS == iota((s.channels * ROWS, s.channels), 1), 1.0, 0.0
    ).astype(BF16)
    pick = jnp.where(iota((3, lanes), 1) // WIN == iota((3, lanes), 0), 1.0, 0.0)
    fetch[0].wait()
    flat = jnp.zeros((s.channels * ROWS, lanes), F32)
    for row_shift in range(3):
        spread = dot(conv_weight[row_shift].astype(F32), pick, ((0,), (0,))).astype(BF16)
        flat = jnp.where(h == u - row_shift + 2, dot(owner, spread), flat)
    table[...] = flat.astype(BF16)
    left = flat.T[: 3 * WIN].astype(BF16)
    for k in range(s.steps):
        if k % (s.steps // parts) == 0:
            fetch[slow + k // (s.steps // parts)].wait()
        block = features[:, k * ROWS : (k + 1) * ROWS, :].reshape(s.channels * ROWS, s.cols)
        for n in range(0, s.cols, 128):
            sums = dot(left, block[:, n : n + 128])
            for b in range(3):
                acc[b, k * ROWS : k * ROWS + WIN, n : n + 128] += sums[b * WIN : (b + 1) * WIN]
    for copy in fetch[1:slow]:
        copy.wait()
    for k in range(s.filters // 2):
        weights_out[k : k + 1, :] = jnp.broadcast_to(weights[k], (1, 128))
    across, down = s.cols // BLOCK, s.rows // BLOCK
    row, col = iota((8, s.width), 0), iota((8, s.width), 1) - s.mask_halo
    inside = (col >= 0) & (col < s.cols) & (row < down)
    number = jnp.where(inside, row * across + (col + BLOCK) // BLOCK - 1, -1)
    used = jnp.zeros((8, s.width), F32)
    for n in range(listed.shape[2]):
        used = jnp.where(number == listed[0, 0, n], 1.0, used)
    own[...] = used
    whole = jnp.zeros((s.grad_pad, s.width), F32)
    blank = jnp.zeros((s.grad_pad, s.width - s.cols), F32)
    for b in range(3):
        part = jnp.concatenate([acc[b, : s.grad_pad], blank], 1)
        whole += pltpu.roll(part, s.base + 2 - b, 1)
    partial[...] = whole

    place, row = iota((s.grad_pad, 128), 1), iota((s.grad_pad, 128), 0)
    filler = jnp.zeros((s.grad_pad - s.rows, 128), F32)
    strips = []
    for first, first_aim, block_col in (
        (s.base, 0, 0),
        (s.cols, s.cols - s.field_halo, across - 1),
    ):
        logits, wanted = pulled_tile(whole, first, 0), pulled_tile(target[...], first_aim, s.strip)
        wanted = jnp.concatenate([wanted, filler], 0)
        number = (row // BLOCK) * across + block_col
        used = jnp.zeros((s.grad_pad, 128), F32)
        for n in range(listed.shape[2]):
            used = jnp.where(number == listed[0, 0, n], 1.0, used)
        used = jnp.where(row < s.rows, used, 0.0)
        value = jnp.where(place < s.strip, logits, wanted)
        value = jnp.where(place < s.strip + s.field_halo, value, used)
        value = jnp.where(place < s.strip + s.field_halo + 1, value, 0.0)
        strips.append(
            jnp.where(iota((s.fold, 128), 1) < 64, value[: s.fold], pltpu.roll(value[s.fold :], 64, 1))
        )
    odd = neighbours("col")[2]
    first_out[...] = jnp.where(odd, strips[0], strips[1])
    second_out[...] = jnp.where(odd, strips[1], strips[0])


def unfolded(s, value):
    low = iota((s.fold, 128), 1) < 64
    return jnp.concatenate(
        [jnp.where(low, value, 0.0), jnp.where(low, pltpu.roll(value, 64, 1), 0.0)], 0
    )


def middle_kernel(s, own_used, partial, target, first, second, band, logits, aim, occupied, first_out, second_out):
    lane = iota((s.grad_pad, 128), 1)
    has_left, has_right, odd = neighbours("col")
    one, two = first[...], second[...]
    west = unfolded(s, jnp.where(has_left, jnp.where(odd, one, two), 0.0))
    east = unfolded(s, jnp.where(has_right, jnp.where(odd, two, one), 0.0))

    def placed(value, keep_from, keep, offset):
        kept = jnp.where((lane >= keep_from) & (lane < keep_from + keep), value, 0.0)
        shift = (offset - keep_from) % 128
        kept = pltpu.roll(kept, shift, 1) if shift else kept
        blank = jnp.zeros((s.grad_pad, 128), F32)
        return jnp.concatenate([kept if n == offset // 128 else blank for n in range(s.width // 128)], 1)

    whole = partial[...] + placed(west, 0, s.strip, 0)
    whole += placed(east, 0, s.strip, s.cols + s.base)
    logits[...] = whole
    own = jnp.concatenate([target[...], jnp.zeros((s.rows, s.width - s.cols), F32)], 1)
    aims = pltpu.roll(own, s.field_halo, 1)
    aims += placed(west, s.strip, s.field_halo, 0)[: s.rows]
    aims += placed(east, s.strip, s.field_halo, s.cols + s.field_halo)[: s.rows]
    aim[...] = aims

    down = s.rows // BLOCK
    row, col = iota((8, s.width), 0), iota((8, s.width), 1) - s.mask_halo
    used = own_used[...]
    flag = s.strip + s.field_halo
    for r in range(down):
        here = row == r
        used = jnp.where(here & (col < 0), west[r * BLOCK : r * BLOCK + 1, flag : flag + 1], used)
        beyond = here & (col >= s.cols) & (col < s.cols + s.mask_halo)
        used = jnp.where(beyond, east[r * BLOCK : r * BLOCK + 1, flag : flag + 1], used)
    occupied[...] = used

    odd = neighbours("row")[2]

    def fill(out, low):
        start = s.rows + 2 - s.strip if low else 0
        start_aim = s.rows - s.field_halo if low else 0
        block_row = down - 1 if low else 0
        out[...] = jnp.zeros_like(out)
        out[: s.strip, :] = whole[start : start + s.strip]
        out[s.strip : s.strip + 1, :] = used[block_row : block_row + 1]
        out[s.strip + 1 : s.strip + 1 + s.field_halo, :] = aims[start_aim : start_aim + s.field_halo]

    @pl.when(odd)
    def _():
        fill(first_out, False)
        fill(second_out, True)

    @pl.when(jnp.logical_not(odd))
    def _():
        fill(first_out, True)
        fill(second_out, False)


def overlapped(s, value):
    return jnp.concatenate([value[:, : s.main], pltpu.roll(value, s.reach, 1)[:, s.main :]], 1)


def optics_kernel(
    s, weights, logits, aim, occupied, first, second, row_band, fwd_main, fwd_last, adj_main, adj_last, adj_high, adj_low,
    features, shifted, terms,
    ext, aims, masks, field, pulled, total,
):

    has_left, has_right, _ = neighbours("col")
    has_up, has_down, odd = neighbours("row")
    one, two = first[...], second[...]
    north = jnp.where(has_up, jnp.where(odd, one, two), 0.0)
    south = jnp.where(has_down, jnp.where(odd, two, one), 0.0)
    edge = up(s.strip, 8)
    lane_row = iota((edge, s.width), 0)
    ext[...] = jnp.zeros_like(ext)
    ext[s.base : s.base + s.grad_pad, :] = logits[...]
    ext[:edge, :] += jnp.where(lane_row < s.strip, north[:edge], 0.0)
    low = s.rows + s.base
    ext[low : low + edge, :] += jnp.where(lane_row < s.strip, south[:edge], 0.0)
    aims[...] = jnp.zeros_like(aims)
    aims[: s.field_halo, :] = north[s.strip + 1 : s.strip + 1 + s.field_halo]
    aims[s.field_halo : s.field_halo + s.rows, :] = aim[...]
    aims[s.field_halo + s.rows : s.field_rows, :] = south[s.strip + 1 : s.strip + 1 + s.field_halo]

    place = iota((s.mask_pad, s.width), 0) - s.mask_halo
    used = jnp.where(place < 0, north[s.strip : s.strip + 1], 0.0)
    for r in range(s.rows // BLOCK):
        used = jnp.where((place >= r * BLOCK) & (place < (r + 1) * BLOCK), occupied[r : r + 1, :], used)
    below = (place >= s.rows) & (place < s.rows + s.mask_halo)
    used = jnp.where(below, south[s.strip : s.strip + 1], used)
    sigma = jax.nn.sigmoid(ext[...])
    mask = used * sigma
    high, low = split(overlapped(s, mask))
    for first_row in (0, s.depth):
        here = slice(first_row, first_row + s.mask_pad)
        masks[here, : s.width] = high
        masks[here, s.width :] = low
        if s.mask_pad < s.depth:
            masks[first_row + s.mask_pad : first_row + s.depth, :] = jnp.zeros(
                (s.depth - s.mask_pad, 2 * s.width), BF16
            )
    slope = (mask * (1.0 - sigma))[s.base : s.base + s.grad_pad]
    slope = pltpu.roll(slope, s.width - s.base, 1)

    total[...] = jnp.zeros_like(total)
    group = 2
    tall = group * s.field_pad
    late = iota((s.field_pad, 128), 1) >= 128 - s.reach

    def banded(high, low, main, last):
        ends = jnp.concatenate([high[:, s.main :], low[:, s.main :]], 1)
        both = dot(ends, jnp.concatenate([last, last], 0))
        tail = both[:, :128] + both[:, 128:]
        high, low = high[:, : s.main], low[:, : s.main]
        rows = high.shape[0]
        both = dot(jnp.concatenate([high, low], 0), main[0])
        head = both[:rows] + both[rows:] + dot(high, main[1])
        seam = head[:, s.main - 128 :] + jnp.where(late, tail, 0.0)
        pieces = [seam, tail]
        if s.main > 128:
            pieces.insert(0, head[:, : s.main - 128])
        return jnp.concatenate(pieces, 1)

    for g in range(s.filters // group):
        band = row_band[g * tall : (g + 1) * tall, :]
        top, bottom = band[:, : s.depth], band[:, s.depth :]
        one = dot(top, masks[: s.depth, :])
        two = dot(bottom, masks[: s.depth, : s.width])
        rowed = one[:, : s.width] + one[:, s.width :] + two
        for i in range(0, group, 2):
            squares = 0.0
            for j in (i, i + 1):
                f = g * group + j
                high, low = split(rowed[j * s.field_pad : (j + 1) * s.field_pad])
                value = banded(high, low, fwd_main[f], fwd_last[f])
                field[f] = value
                squares += value * value
            k = (g * group + i) // 2
            total[...] += squares * weights[k : k + 1, :1]

    row, lane = iota((s.field_pad, s.width), 0) - s.field_halo, iota((s.field_pad, s.width), 1)
    col = jnp.where(lane < s.main, lane, lane - s.reach) - s.field_halo
    inside = ((row >= 0) | has_up) & ((row < s.rows) | has_down) & (row < s.rows + s.field_halo)
    inside &= ((col >= 0) | has_left) & ((col < s.cols) | has_right) & (col < s.cols + s.field_halo)
    total[...] = jnp.where(inside, total[...] - overlapped(s, aims[...]), 0.0)

    for f in range(s.filters):
        high, low = split(total[...] * field[f])
        high, low = split(banded(high, low, adj_main[f], adj_last[f]))
        rows = slice(f * s.field_pad, (f + 1) * s.field_pad)
        pulled[rows, : s.width] = high
        pulled[rows, s.width : s.width + 128] = low[:, s.main :]
        pulled[rows, s.width + 128 :] = low[:, : s.main]

    both = dot(jnp.concatenate([adj_high[...], adj_low[...]], 0), pulled[:, : s.width + 128])
    rest = both[: s.grad_pad, s.width :]
    both = both[: s.grad_pad, : s.width] + both[s.grad_pad :, : s.width]
    low = dot(adj_high[...], pulled[:, s.width + 128 :])
    grad = jnp.concatenate([both[:, : s.main] + low, both[:, s.main :] + rest], 1) * slope

    for b in range(3):
        moved = grad if b == 2 else pltpu.roll(grad, s.width - (2 - b), 1)
        moved = moved[:, : s.cols]
        shifted[b], shifted[3 + b] = split(moved)
        rest = moved - shifted[b].astype(F32) - shifted[3 + b].astype(F32)
        shifted[6 + b] = rest.astype(BF16)
    sums = jnp.zeros((s.channels * ROWS, 6 * WIN), F32)
    for k in range(s.steps):
        block = features[:, k * ROWS : (k + 1) * ROWS, :].reshape(s.channels * ROWS, s.cols)
        window = jnp.concatenate([shifted[q, k * ROWS : k * ROWS + WIN, :] for q in range(6)], 0)
        sums += dot(block, window, NT)
    cube = sums.reshape(s.channels, ROWS, 6 * WIN)
    u, lane = iota((ROWS, 6 * WIN), 0), iota((ROWS, 6 * WIN), 1)
    number, group = iota((16, 6 * WIN), 0), (iota((16, 6 * WIN), 1) // WIN) % 3
    result = jnp.zeros((16, s.channels), F32)
    for a in range(3):
        hit = jnp.where(lane % WIN == u - a + 2, 1.0, 0.0)
        line = (cube * hit[None]).sum(1)
        pick = jnp.where(number == a * 3 + group, 1.0, 0.0)
        result += dot(pick, line, NT, lax.Precision.HIGHEST)
    terms[...] = result


def feature_kernel(s, table, shifted, out, blocks, sems):
    copies = []
    wide = jnp.concatenate([table[...]] * 3, 1)
    blank = jnp.zeros((WIN, s.cols), BF16)
    for k in range(s.steps):
        rows = slice(k * ROWS, k * ROWS + WIN)
        parts = []
        for part in range(3):
            parts += [shifted[3 * part + b, rows, :] for b in range(3)] + [blank]
        value = dot(wide, jnp.concatenate(parts, 0))
        here = pl.ds(k * ROWS, ROWS)
        blocks[:, here, :] = value.astype(BF16).reshape(s.channels, ROWS, s.cols)
        copies.append(pltpu.make_async_copy(blocks.at[:, here, :], out.at[:, here, :], sems.at[k]))
        copies[-1].start()
    for copy in copies:
        copy.wait()


def spec(space=pltpu.VMEM):
    return pl.BlockSpec(memory_space=space)


def exchanged(first, second, axis):
    size, parts = lax.axis_size(axis), lax.axis_size("grp")
    one = lax.ppermute(first, axis, [(i, i ^ 1) for i in range(size)])
    pairs = []
    for g in range(parts):
        for i in range(size):
            j = i + 1 if i % 2 else i - 1
            if 0 <= j < size:
                pairs.append((g * size + i, g * size + j))
            elif parts % 2:
                pairs.append((g * size + i, g * size + (j % size)))
            else:
                pairs.append((g * size + i, (g ^ 1) * size + i))
    return one, lax.ppermute(second, ("grp", axis), pairs)


def summed(value, axis):
    size = lax.axis_size(axis)
    parts = [
        lax.ppermute(value, axis, [(i, i ^ step) for i in range(size)]) for step in range(1, size)
    ]
    return functools.reduce(jnp.add, parts, value)


def on_device(features, conv_weight, row_taps, col_taps, kernel_weight, target, block_list):
    channels, tile_rows, tile_cols = features.shape
    s = Sizes(channels, tile_rows, tile_cols, row_taps.shape[2], row_taps.shape[0] * 2)
    shape = jax.ShapeDtypeStruct
    hbm = spec(pltpu.HBM)

    def call(body, outs, ins, scratch=(), limit=24, out_space=pltpu.VMEM):
        return pl.pallas_call(
            functools.partial(body, s),
            out_shape=outs,
            in_specs=ins,
            out_specs=jax.tree.map(lambda _: spec(out_space), outs),
            scratch_shapes=list(scratch),
            compiler_params=pltpu.CompilerParams(vmem_limit_bytes=limit * MIB),
        )

    half_strip = shape((s.fold, 128), F32)
    table, partial, first, second, features_here, target_here, row_here, col_here, weights, own = call(
        edge_kernel,
        (
            shape((channels * ROWS, 128), BF16),
            shape((s.grad_pad, s.width), F32),
            half_strip,
            half_strip,
            shape(features.shape, BF16),
            shape(target.shape, F32),
            shape(row_taps.shape, F32),
            shape(col_taps.shape, F32),
            shape((8 * -(-s.filters // 16), 128), F32),
            shape((8, s.width), F32),
        ),
        [hbm] * 7,
        [
            pltpu.VMEM((3, s.rows + WIN, s.cols), F32),
            pltpu.SMEM(block_list.shape, jnp.int32),
            pltpu.VMEM((3, 3, channels), BF16),
            pltpu.SMEM(kernel_weight.shape, F32),
            pltpu.SemaphoreType.DMA((10,)),
        ],
    )(
        *(
            pltpu.with_memory_space_constraint(x, pltpu.HBM)
            for x in (
                block_list, features, conv_weight.transpose(1, 2, 0), target, row_taps, col_taps,
                kernel_weight,
            )
        )
    )
    first, second = exchanged(first, second, "col")

    filters = s.filters
    col_bands = call(
        col_band_kernel,
        (shape((filters, 2, s.main, s.main), BF16), shape((filters, 128, 256), BF16)) * 2,
        [spec()],
    )(col_here)
    row_bands = call(
        row_band_kernel,
        (
            shape((filters * s.field_pad, 2 * s.depth), BF16),
            shape((s.grad_pad, filters * s.field_pad), BF16),
            shape((s.grad_pad, filters * s.field_pad), BF16),
        ),
        [spec(), spec()],
        [pltpu.VMEM((filters * s.field_pad, s.depth), F32)],
    )(row_here, weights)

    row_strip = shape((s.strip_rows, s.width), F32)
    logits, aim, occupied, first, second = call(
        middle_kernel,
        (
            shape((s.grad_pad, s.width), F32),
            shape((s.rows, s.width), F32),
            shape((8, s.width), F32),
            row_strip,
            row_strip,
        ),
        [spec()] * 6,
    )(own, partial, target_here, first, second, col_bands[1])
    first, second = exchanged(first, second, "row")

    shifted, terms = call(
        optics_kernel,
        (shape((9, s.grad_pad, s.cols), BF16), shape((16, channels), F32)),
        [spec()] * 14,
        [
            pltpu.VMEM((s.mask_pad, s.width), F32),
            pltpu.VMEM((s.field_pad, s.width), F32),
            pltpu.VMEM((2 * s.depth, 2 * s.width), BF16),
            pltpu.VMEM((filters, s.field_pad, s.width), F32),
            pltpu.VMEM((filters * s.field_pad, 2 * s.width), BF16),
            pltpu.VMEM((s.field_pad, s.width), F32),
        ],
        32,
    )(weights, logits, aim, occupied, first, second, *row_bands[:1], *col_bands, *row_bands[1:], features_here)

    by_row = summed(terms, "row")
    grad_features = call(
        feature_kernel,
        shape(features.shape, BF16),
        [spec(), spec()],
        [pltpu.VMEM(features.shape, BF16), pltpu.SemaphoreType.DMA((s.steps,))],
        out_space=pltpu.HBM,
    )(table, shifted)
    whole = summed(by_row, "col")
    height = tile_rows * lax.axis_size("row")
    width = tile_cols * lax.axis_size("col")
    grad_weight = (whole[:9].T / math.sqrt(height * width)).reshape(channels, 3, 3)
    return (grad_weight, grad_features)


def solution(mesh):
    placed = (
        P(None, ("grp", "row"), "col"),
        P(),
        P(),
        P(),
        P(),
        P(("grp", "row"), "col"),
        P(("grp", "row"), "col", None),
    )
    return jax.shard_map(
        on_device,
        mesh=mesh,
        in_specs=placed,
        out_specs=(P("grp", None, None), P(None, ("grp", "row"), "col")),
        check_vma=False,
    )
```

```python
import functools
import math

import jax
import jax.numpy as jnp
from jax import lax
from jax.experimental import pallas as pl
from jax.experimental.pallas import tpu as pltpu
from jax.sharding import PartitionSpec as P

BLOCK = 64
ROWS = 16
WIN = 32
MIB = 1 << 20
F32 = jnp.float32
BF16 = jnp.bfloat16


def up(value, multiple):
    return -(-value // multiple) * multiple


def iota(shape, dim):
    return lax.broadcasted_iota(jnp.int32, shape, dim)


def split(value):
    high = value.astype(BF16)
    return high, (value - high.astype(F32)).astype(BF16)


def dot(left, right, dims=((1,), (0,)), precision=None):
    return lax.dot_general(
        left, right, (dims, ((), ())), precision=precision, preferred_element_type=F32
    )


NT = ((1,), (1,))


def neighbours(axis):
    here = lax.axis_index(axis)
    return here > 0, here < lax.axis_size(axis) - 1, here % 2 == 1


class Sizes:
    def __init__(self, channels, tile_rows, tile_cols, taps, filters):
        self.channels, self.rows, self.cols = channels, tile_rows, tile_cols
        self.taps, self.filters = taps, filters
        self.half = (taps - 1) // 2
        self.mask_halo = 2 * self.half + 1
        self.field_halo = self.half + 1
        self.strip = self.mask_halo + 1
        self.base = self.mask_halo - 1
        self.width = up(tile_cols + 2 * self.mask_halo, 128)
        self.field_rows = tile_rows + 2 * self.field_halo
        self.field_cols = tile_cols + 2 * self.field_halo
        self.field_pad = up(self.field_rows, 16)
        self.grad_pad = tile_rows + ROWS
        mask_rows = tile_rows + 2 * self.mask_halo
        self.mask_pad = up(mask_rows, 16)
        self.depth = up(max(mask_rows, self.field_pad + taps), 128)
        self.steps = tile_rows // ROWS
        self.reach = taps - 1
        self.main = self.width - 128
        self.strip_rows = up(self.strip + 1 + self.field_halo, 8)
        self.fold = self.grad_pad // 2


def row_band_kernel(s, row_taps, weights, row_band, adj_high, adj_low, flipped):
    for f in range(s.filters):
        k, p = f // 2, f % 2
        pad = jnp.zeros((1, s.depth - s.taps), F32)
        row = jnp.concatenate([row_taps[k, p : p + 1, :], pad], 1)
        band = pltpu.roll(
            jnp.broadcast_to(row, (s.field_pad, s.depth)), 0, 1, stride=1, stride_axis=0
        )
        here = slice(f * s.field_pad, (f + 1) * s.field_pad)
        row_band[here, : s.depth], row_band[here, s.depth :] = split(band)
        flipped[here, :] = pltpu.roll(
            jnp.broadcast_to(row * (2.0 * weights[k : k + 1, :1]), (s.field_pad, s.depth)),
            s.depth - s.reach,
            1,
            stride=1,
            stride_axis=0,
        )
    turned = flipped[...].T[: s.grad_pad, :]
    adj_high[...], adj_low[...] = split(turned)


def col_band_kernel(s, col_taps, fwd_main, fwd_last, adj_main, adj_last):
    early = iota((128, 128), 1) < 128 - s.reach
    blocks = s.main // 128
    blank = jnp.zeros((128, 128), BF16)

    def fill(out, f, same, below):
        ends = split(jnp.where(early, same, 0.0))
        same, below = split(same), split(below)
        for part in range(2):
            for i in range(blocks):
                for j in range(blocks):
                    piece = blank
                    if i == j:
                        piece = ends[part] if j == blocks - 1 else same[part]
                    elif i == j + 1:
                        piece = below[part]
                    out[f, part, 128 * i : 128 * (i + 1), 128 * j : 128 * (j + 1)] = piece

    for f in range(s.filters):
        k, p = f // 2, f % 2
        pad = jnp.zeros((1, 256 - s.taps), F32)
        wide = jnp.concatenate([col_taps[k, p : p + 1, :], pad], 1)
        band = pltpu.roll(jnp.broadcast_to(wide, (128, 256)), 0, 1, stride=1, stride_axis=0)
        turned = band.T
        fill(fwd_main, f, turned[:128], turned[128:])
        corner = jnp.concatenate([band[: 128 - s.reach, :128], band[: s.reach, :128]], 0).T
        fwd_last[f, :, :128], fwd_last[f, :, 128:] = split(corner)
        band = pltpu.roll(
            jnp.broadcast_to(wide, (256, 256)), 256 - s.reach, 1, stride=1, stride_axis=0
        )[:, :128]
        fill(adj_main, f, band[:128], band[128:])
        corner = pltpu.roll(
            jnp.broadcast_to(wide[:, :128], (128, 128)), 128 - 2 * s.reach, 1, stride=1, stride_axis=0
        )
        adj_last[f, :, :128], adj_last[f, :, 128:] = split(corner)


def pulled_tile(value, start, lane):
    first = start // 128 * 128
    tile = value[:, first : first + 128]
    shift = (lane - start) % 128
    return pltpu.roll(tile, shift, 1) if shift else tile


def edge_kernel(
    s, listed_hbm, features_hbm, conv_weight_hbm, target_hbm, row_taps_hbm, col_taps_hbm, weights_hbm,
    table, acc, first_out, second_out, features, target, row_taps, col_taps, weights_out, own,
    listed, conv_weight, weights, sems,
):
    fetch = [
        pltpu.make_async_copy(conv_weight_hbm, conv_weight, sems.at[0]),
        pltpu.make_async_copy(listed_hbm, listed, sems.at[1]),
        pltpu.make_async_copy(target_hbm, target, sems.at[2]),
        pltpu.make_async_copy(row_taps_hbm, row_taps, sems.at[7]),
        pltpu.make_async_copy(col_taps_hbm, col_taps, sems.at[8]),
        pltpu.make_async_copy(weights_hbm, weights, sems.at[9]),
    ]
    slow = len(fetch)
    parts = 4
    rows = s.rows // parts
    for q in range(parts):
        here = pl.ds(q * rows, rows)
        fetch.append(
            pltpu.make_async_copy(features_hbm.at[:, here, :], features.at[:, here, :], sems.at[3 + q])
        )
    for copy in fetch:
        copy.start()
    acc[...] = jnp.zeros_like(acc)
    lanes = 128
    u, lane = iota((s.channels * ROWS, lanes), 0) % ROWS, iota((s.channels * ROWS, lanes), 1)
    h = lane % WIN
    owner = jnp.where(
        iota((s.channels * ROWS, s.channels), 0) // ROWS == iota((s.channels * ROWS, s.channels), 1), 1.0, 0.0
    ).astype(BF16)
    pick = jnp.where(iota((3, lanes), 1) // WIN == iota((3, lanes), 0), 1.0, 0.0)
    fetch[0].wait()
    flat = jnp.zeros((s.channels * ROWS, lanes), F32)
    for row_shift in range(3):
        spread = dot(conv_weight[row_shift].astype(F32), pick, ((0,), (0,))).astype(BF16)
        flat = jnp.where(h == u - row_shift + 2, dot(owner, spread), flat)
    table[...] = flat.astype(BF16)
    left = flat.T[: 3 * WIN].astype(BF16)
    for k in range(s.steps):
        if k % (s.steps // parts) == 0:
            fetch[slow + k // (s.steps // parts)].wait()
        block = features[:, k * ROWS : (k + 1) * ROWS, :].reshape(s.channels * ROWS, s.cols)
        for n in range(0, s.cols, 128):
            sums = dot(left, block[:, n : n + 128])
            for b in range(3):
                acc[b, k * ROWS : k * ROWS + WIN, n : n + 128] += sums[b * WIN : (b + 1) * WIN]
    for copy in fetch[1:slow]:
        copy.wait()
    for k in range(s.filters // 2):
        weights_out[k : k + 1, :] = jnp.broadcast_to(weights[k], (1, 128))
    across, down = s.cols // BLOCK, s.rows // BLOCK
    row, col = iota((8, s.width), 0), iota((8, s.width), 1) - s.mask_halo
    inside = (col >= 0) & (col < s.cols) & (row < down)
    number = jnp.where(inside, row * across + (col + BLOCK) // BLOCK - 1, -1)
    used = jnp.zeros((8, s.width), F32)
    for n in range(listed.shape[2]):
        used = jnp.where(number == listed[0, 0, n], 1.0, used)
    own[...] = used
    place, row = iota((s.grad_pad, 128), 1), iota((s.grad_pad, 128), 0)
    filler = jnp.zeros((s.grad_pad - s.rows, 128), F32)
    strips = []
    for first_aim, block_col in ((0, 0), (s.cols - s.field_halo, across - 1)):
        logits = jnp.zeros((s.grad_pad, 128), F32)
        for b in range(3):
            if block_col == 0:
                part = acc[b, : s.grad_pad, :128]
                shift, kept = 2 - b, place >= 2 - b
            else:
                part = acc[b, : s.grad_pad, s.cols - 128 :]
                shift, kept = s.strip - b, place < s.strip - b
            part = pltpu.roll(part, shift, 1) if shift else part
            logits += jnp.where(kept, part, 0.0)
        wanted = pulled_tile(target[...], first_aim, s.strip)
        wanted = jnp.concatenate([wanted, filler], 0)
        number = (row // BLOCK) * across + block_col
        used = jnp.zeros((s.grad_pad, 128), F32)
        for n in range(listed.shape[2]):
            used = jnp.where(number == listed[0, 0, n], 1.0, used)
        used = jnp.where(row < s.rows, used, 0.0)
        value = jnp.where(place < s.strip, logits, wanted)
        value = jnp.where(place < s.strip + s.field_halo, value, used)
        value = jnp.where(place < s.strip + s.field_halo + 1, value, 0.0)
        strips.append(
            jnp.where(iota((s.fold, 128), 1) < 64, value[: s.fold], pltpu.roll(value[s.fold :], 64, 1))
        )
    odd = neighbours("col")[2]
    first_out[...] = jnp.where(odd, strips[0], strips[1])
    second_out[...] = jnp.where(odd, strips[1], strips[0])


def partial_kernel(s, acc, partial):
    whole = jnp.zeros((s.grad_pad, s.width), F32)
    blank = jnp.zeros((s.grad_pad, s.width - s.cols), F32)
    for b in range(3):
        part = jnp.concatenate([acc[b, : s.grad_pad], blank], 1)
        whole += pltpu.roll(part, s.base + 2 - b, 1)
    partial[...] = whole


def unfolded(s, value):
    low = iota((s.fold, 128), 1) < 64
    return jnp.concatenate(
        [jnp.where(low, value, 0.0), jnp.where(low, pltpu.roll(value, 64, 1), 0.0)], 0
    )


def middle_kernel(s, own_used, partial, target, first, second, band, logits, aim, occupied, first_out, second_out):
    lane = iota((s.grad_pad, 128), 1)
    has_left, has_right, odd = neighbours("col")
    one, two = first[...], second[...]
    west = unfolded(s, jnp.where(has_left, jnp.where(odd, one, two), 0.0))
    east = unfolded(s, jnp.where(has_right, jnp.where(odd, two, one), 0.0))

    def placed(value, keep_from, keep, offset):
        kept = jnp.where((lane >= keep_from) & (lane < keep_from + keep), value, 0.0)
        shift = (offset - keep_from) % 128
        kept = pltpu.roll(kept, shift, 1) if shift else kept
        blank = jnp.zeros((s.grad_pad, 128), F32)
        return jnp.concatenate([kept if n == offset // 128 else blank for n in range(s.width // 128)], 1)

    whole = partial[...] + placed(west, 0, s.strip, 0)
    whole += placed(east, 0, s.strip, s.cols + s.base)
    logits[...] = whole
    own = jnp.concatenate([target[...], jnp.zeros((s.rows, s.width - s.cols), F32)], 1)
    aims = pltpu.roll(own, s.field_halo, 1)
    aims += placed(west, s.strip, s.field_halo, 0)[: s.rows]
    aims += placed(east, s.strip, s.field_halo, s.cols + s.field_halo)[: s.rows]
    aim[...] = aims

    down = s.rows // BLOCK
    row, col = iota((8, s.width), 0), iota((8, s.width), 1) - s.mask_halo
    used = own_used[...]
    flag = s.strip + s.field_halo
    for r in range(down):
        here = row == r
        used = jnp.where(here & (col < 0), west[r * BLOCK : r * BLOCK + 1, flag : flag + 1], used)
        beyond = here & (col >= s.cols) & (col < s.cols + s.mask_halo)
        used = jnp.where(beyond, east[r * BLOCK : r * BLOCK + 1, flag : flag + 1], used)
    occupied[...] = used

    odd = neighbours("row")[2]

    def fill(out, low):
        start = s.rows + 2 - s.strip if low else 0
        start_aim = s.rows - s.field_halo if low else 0
        block_row = down - 1 if low else 0
        out[...] = jnp.zeros_like(out)
        out[: s.strip, :] = whole[start : start + s.strip]
        out[s.strip : s.strip + 1, :] = used[block_row : block_row + 1]
        out[s.strip + 1 : s.strip + 1 + s.field_halo, :] = aims[start_aim : start_aim + s.field_halo]

    @pl.when(odd)
    def _():
        fill(first_out, False)
        fill(second_out, True)

    @pl.when(jnp.logical_not(odd))
    def _():
        fill(first_out, True)
        fill(second_out, False)


def overlapped(s, value):
    return jnp.concatenate([value[:, : s.main], pltpu.roll(value, s.reach, 1)[:, s.main :]], 1)


def optics_kernel(
    s, weights, logits, aim, occupied, first, second, row_band, fwd_main, fwd_last, adj_main, adj_last, adj_high, adj_low,
    features, shifted, terms,
    ext, aims, masks, field, pulled, total,
):

    has_left, has_right, _ = neighbours("col")
    has_up, has_down, odd = neighbours("row")
    one, two = first[...], second[...]
    north = jnp.where(has_up, jnp.where(odd, one, two), 0.0)
    south = jnp.where(has_down, jnp.where(odd, two, one), 0.0)
    edge = up(s.strip, 8)
    lane_row = iota((edge, s.width), 0)
    ext[...] = jnp.zeros_like(ext)
    ext[s.base : s.base + s.grad_pad, :] = logits[...]
    ext[:edge, :] += jnp.where(lane_row < s.strip, north[:edge], 0.0)
    low = s.rows + s.base
    ext[low : low + edge, :] += jnp.where(lane_row < s.strip, south[:edge], 0.0)
    aims[...] = jnp.zeros_like(aims)
    aims[: s.field_halo, :] = north[s.strip + 1 : s.strip + 1 + s.field_halo]
    aims[s.field_halo : s.field_halo + s.rows, :] = aim[...]
    aims[s.field_halo + s.rows : s.field_rows, :] = south[s.strip + 1 : s.strip + 1 + s.field_halo]

    place = iota((s.mask_pad, s.width), 0) - s.mask_halo
    used = jnp.where(place < 0, north[s.strip : s.strip + 1], 0.0)
    for r in range(s.rows // BLOCK):
        used = jnp.where((place >= r * BLOCK) & (place < (r + 1) * BLOCK), occupied[r : r + 1, :], used)
    below = (place >= s.rows) & (place < s.rows + s.mask_halo)
    used = jnp.where(below, south[s.strip : s.strip + 1], used)
    sigma = jax.nn.sigmoid(ext[...])
    mask = used * sigma
    high, low = split(overlapped(s, mask))
    for first_row in (0, s.depth):
        here = slice(first_row, first_row + s.mask_pad)
        masks[here, : s.width] = high
        masks[here, s.width :] = low
        if s.mask_pad < s.depth:
            masks[first_row + s.mask_pad : first_row + s.depth, :] = jnp.zeros(
                (s.depth - s.mask_pad, 2 * s.width), BF16
            )
    slope = (mask * (1.0 - sigma))[s.base : s.base + s.grad_pad]
    slope = pltpu.roll(slope, s.width - s.base, 1)

    total[...] = jnp.zeros_like(total)
    group = 2
    tall = group * s.field_pad
    late = iota((s.field_pad, 128), 1) >= 128 - s.reach

    def banded(high, low, main, last):
        ends = jnp.concatenate([high[:, s.main :], low[:, s.main :]], 1)
        both = dot(ends, jnp.concatenate([last, last], 0))
        tail = both[:, :128] + both[:, 128:]
        high, low = high[:, : s.main], low[:, : s.main]
        rows = high.shape[0]
        both = dot(jnp.concatenate([high, low], 0), main[0])
        head = both[:rows] + both[rows:] + dot(high, main[1])
        seam = head[:, s.main - 128 :] + jnp.where(late, tail, 0.0)
        pieces = [seam, tail]
        if s.main > 128:
            pieces.insert(0, head[:, : s.main - 128])
        return jnp.concatenate(pieces, 1)

    for g in range(s.filters // group):
        band = row_band[g * tall : (g + 1) * tall, :]
        top, bottom = band[:, : s.depth], band[:, s.depth :]
        one = dot(top, masks[: s.depth, :])
        two = dot(bottom, masks[: s.depth, : s.width])
        rowed = one[:, : s.width] + one[:, s.width :] + two
        for i in range(0, group, 2):
            squares = 0.0
            for j in (i, i + 1):
                f = g * group + j
                high, low = split(rowed[j * s.field_pad : (j + 1) * s.field_pad])
                value = banded(high, low, fwd_main[f], fwd_last[f])
                field[f] = value
                squares += value * value
            k = (g * group + i) // 2
            total[...] += squares * weights[k : k + 1, :1]

    row, lane = iota((s.field_pad, s.width), 0) - s.field_halo, iota((s.field_pad, s.width), 1)
    col = jnp.where(lane < s.main, lane, lane - s.reach) - s.field_halo
    inside = ((row >= 0) | has_up) & ((row < s.rows) | has_down) & (row < s.rows + s.field_halo)
    inside &= ((col >= 0) | has_left) & ((col < s.cols) | has_right) & (col < s.cols + s.field_halo)
    total[...] = jnp.where(inside, total[...] - overlapped(s, aims[...]), 0.0)

    for f in range(s.filters):
        high, low = split(total[...] * field[f])
        high, low = split(banded(high, low, adj_main[f], adj_last[f]))
        rows = slice(f * s.field_pad, (f + 1) * s.field_pad)
        pulled[rows, : s.width] = high
        pulled[rows, s.width : s.width + 128] = low[:, s.main :]
        pulled[rows, s.width + 128 :] = low[:, : s.main]

    both = dot(jnp.concatenate([adj_high[...], adj_low[...]], 0), pulled[:, : s.width + 128])
    rest = both[: s.grad_pad, s.width :]
    both = both[: s.grad_pad, : s.width] + both[s.grad_pad :, : s.width]
    low = dot(adj_high[...], pulled[:, s.width + 128 :])
    grad = jnp.concatenate([both[:, : s.main] + low, both[:, s.main :] + rest], 1) * slope

    for b in range(3):
        moved = grad if b == 2 else pltpu.roll(grad, s.width - (2 - b), 1)
        moved = moved[:, : s.cols]
        shifted[b], shifted[3 + b] = split(moved)
        rest = moved - shifted[b].astype(F32) - shifted[3 + b].astype(F32)
        shifted[6 + b] = rest.astype(BF16)
    sums = jnp.zeros((s.channels * ROWS, 6 * WIN), F32)
    for k in range(s.steps):
        block = features[:, k * ROWS : (k + 1) * ROWS, :].reshape(s.channels * ROWS, s.cols)
        window = jnp.concatenate([shifted[q, k * ROWS : k * ROWS + WIN, :] for q in range(6)], 0)
        sums += dot(block, window, NT)
    cube = sums.reshape(s.channels, ROWS, 6 * WIN)
    u, lane = iota((ROWS, 6 * WIN), 0), iota((ROWS, 6 * WIN), 1)
    number, group = iota((16, 6 * WIN), 0), (iota((16, 6 * WIN), 1) // WIN) % 3
    result = jnp.zeros((16, s.channels), F32)
    for a in range(3):
        hit = jnp.where(lane % WIN == u - a + 2, 1.0, 0.0)
        line = (cube * hit[None]).sum(1)
        pick = jnp.where(number == a * 3 + group, 1.0, 0.0)
        result += dot(pick, line, NT, lax.Precision.HIGHEST)
    terms[...] = result


def feature_kernel(s, table, shifted, out, blocks, sems):
    copies = []
    wide = jnp.concatenate([table[...]] * 3, 1)
    blank = jnp.zeros((WIN, s.cols), BF16)
    for k in range(s.steps):
        rows = slice(k * ROWS, k * ROWS + WIN)
        parts = []
        for part in range(3):
            parts += [shifted[3 * part + b, rows, :] for b in range(3)] + [blank]
        value = dot(wide, jnp.concatenate(parts, 0))
        here = pl.ds(k * ROWS, ROWS)
        blocks[:, here, :] = value.astype(BF16).reshape(s.channels, ROWS, s.cols)
        copies.append(pltpu.make_async_copy(blocks.at[:, here, :], out.at[:, here, :], sems.at[k]))
        copies[-1].start()
    for copy in copies:
        copy.wait()


def spec(space=pltpu.VMEM):
    return pl.BlockSpec(memory_space=space)


def exchanged(first, second, axis):
    size, parts = lax.axis_size(axis), lax.axis_size("grp")
    one = lax.ppermute(first, axis, [(i, i ^ 1) for i in range(size)])
    pairs = []
    for g in range(parts):
        for i in range(size):
            j = i + 1 if i % 2 else i - 1
            if 0 <= j < size:
                pairs.append((g * size + i, g * size + j))
            elif parts % 2:
                pairs.append((g * size + i, g * size + (j % size)))
            else:
                pairs.append((g * size + i, (g ^ 1) * size + i))
    return one, lax.ppermute(second, ("grp", axis), pairs)


def summed(value, axis):
    size = lax.axis_size(axis)
    parts = [
        lax.ppermute(value, axis, [(i, i ^ step) for i in range(size)]) for step in range(1, size)
    ]
    return functools.reduce(jnp.add, parts, value)


def on_device(features, conv_weight, row_taps, col_taps, kernel_weight, target, block_list):
    channels, tile_rows, tile_cols = features.shape
    s = Sizes(channels, tile_rows, tile_cols, row_taps.shape[2], row_taps.shape[0] * 2)
    shape = jax.ShapeDtypeStruct
    hbm = spec(pltpu.HBM)

    def call(body, outs, ins, scratch=(), limit=24, out_space=pltpu.VMEM):
        return pl.pallas_call(
            functools.partial(body, s),
            out_shape=outs,
            in_specs=ins,
            out_specs=jax.tree.map(lambda _: spec(out_space), outs),
            scratch_shapes=list(scratch),
            compiler_params=pltpu.CompilerParams(vmem_limit_bytes=limit * MIB),
        )

    half_strip = shape((s.fold, 128), F32)
    table, sums, first, second, features_here, target_here, row_here, col_here, weights, own = call(
        edge_kernel,
        (
            shape((channels * ROWS, 128), BF16),
            shape((3, s.rows + WIN, s.cols), F32),
            half_strip,
            half_strip,
            shape(features.shape, BF16),
            shape(target.shape, F32),
            shape(row_taps.shape, F32),
            shape(col_taps.shape, F32),
            shape((8 * -(-s.filters // 16), 128), F32),
            shape((8, s.width), F32),
        ),
        [hbm] * 7,
        [
            pltpu.SMEM(block_list.shape, jnp.int32),
            pltpu.VMEM((3, 3, channels), BF16),
            pltpu.SMEM(kernel_weight.shape, F32),
            pltpu.SemaphoreType.DMA((10,)),
        ],
    )(
        *(
            pltpu.with_memory_space_constraint(x, pltpu.HBM)
            for x in (
                block_list, features, conv_weight.transpose(1, 2, 0), target, row_taps, col_taps,
                kernel_weight,
            )
        )
    )
    first, second = exchanged(first, second, "col")
    partial = call(partial_kernel, shape((s.grad_pad, s.width), F32), [spec()])(sums)

    filters = s.filters
    col_bands = call(
        col_band_kernel,
        (shape((filters, 2, s.main, s.main), BF16), shape((filters, 128, 256), BF16)) * 2,
        [spec()],
    )(col_here)
    row_bands = call(
        row_band_kernel,
        (
            shape((filters * s.field_pad, 2 * s.depth), BF16),
            shape((s.grad_pad, filters * s.field_pad), BF16),
            shape((s.grad_pad, filters * s.field_pad), BF16),
        ),
        [spec(), spec()],
        [pltpu.VMEM((filters * s.field_pad, s.depth), F32)],
    )(row_here, weights)

    row_strip = shape((s.strip_rows, s.width), F32)
    logits, aim, occupied, first, second = call(
        middle_kernel,
        (
            shape((s.grad_pad, s.width), F32),
            shape((s.rows, s.width), F32),
            shape((8, s.width), F32),
            row_strip,
            row_strip,
        ),
        [spec()] * 6,
    )(own, partial, target_here, first, second, col_bands[1])
    first, second = exchanged(first, second, "row")

    shifted, terms = call(
        optics_kernel,
        (shape((9, s.grad_pad, s.cols), BF16), shape((16, channels), F32)),
        [spec()] * 14,
        [
            pltpu.VMEM((s.mask_pad, s.width), F32),
            pltpu.VMEM((s.field_pad, s.width), F32),
            pltpu.VMEM((2 * s.depth, 2 * s.width), BF16),
            pltpu.VMEM((filters, s.field_pad, s.width), F32),
            pltpu.VMEM((filters * s.field_pad, 2 * s.width), BF16),
            pltpu.VMEM((s.field_pad, s.width), F32),
        ],
        32,
    )(weights, logits, aim, occupied, first, second, *row_bands[:1], *col_bands, *row_bands[1:], features_here)

    by_row = summed(terms, "row")
    grad_features = call(
        feature_kernel,
        shape(features.shape, BF16),
        [spec(), spec()],
        [pltpu.VMEM(features.shape, BF16), pltpu.SemaphoreType.DMA((s.steps,))],
        out_space=pltpu.HBM,
    )(table, shifted)
    whole = summed(by_row, "col")
    height = tile_rows * lax.axis_size("row")
    width = tile_cols * lax.axis_size("col")
    grad_weight = (whole[:9].T / math.sqrt(height * width)).reshape(channels, 3, 3)
    return (grad_weight, grad_features)


def solution(mesh):
    placed = (
        P(None, ("grp", "row"), "col"),
        P(),
        P(),
        P(),
        P(),
        P(("grp", "row"), "col"),
        P(("grp", "row"), "col", None),
    )
    return jax.shard_map(
        on_device,
        mesh=mesh,
        in_specs=placed,
        out_specs=(P("grp", None, None), P(None, ("grp", "row"), "col")),
        check_vma=False,
    )
```

```python
import functools
import math

import jax
import jax.numpy as jnp
from jax import lax
from jax.experimental import pallas as pl
from jax.experimental.pallas import tpu as pltpu
from jax.sharding import PartitionSpec as P

BLOCK = 64
ROWS = 16
WIN = 32
MIB = 1 << 20
F32 = jnp.float32
BF16 = jnp.bfloat16


def up(value, multiple):
    return -(-value // multiple) * multiple


def iota(shape, dim):
    return lax.broadcasted_iota(jnp.int32, shape, dim)


def split(value):
    high = value.astype(BF16)
    return high, (value - high.astype(F32)).astype(BF16)


def dot(left, right, dims=((1,), (0,)), precision=None):
    return lax.dot_general(
        left, right, (dims, ((), ())), precision=precision, preferred_element_type=F32
    )


NT = ((1,), (1,))


def neighbours(axis):
    here = lax.axis_index(axis)
    return here > 0, here < lax.axis_size(axis) - 1, here % 2 == 1


class Sizes:
    def __init__(self, channels, tile_rows, tile_cols, taps, filters):
        self.channels, self.rows, self.cols = channels, tile_rows, tile_cols
        self.taps, self.filters = taps, filters
        self.half = (taps - 1) // 2
        self.mask_halo = 2 * self.half + 1
        self.field_halo = self.half + 1
        self.strip = self.mask_halo + 1
        self.base = self.mask_halo - 1
        self.width = up(tile_cols + 2 * self.mask_halo, 128)
        self.field_rows = tile_rows + 2 * self.field_halo
        self.field_cols = tile_cols + 2 * self.field_halo
        self.field_pad = up(self.field_rows, 16)
        self.grad_pad = tile_rows + ROWS
        mask_rows = tile_rows + 2 * self.mask_halo
        self.mask_pad = up(mask_rows, 16)
        self.depth = up(max(mask_rows, self.field_pad + taps), 128)
        self.steps = tile_rows // ROWS
        self.reach = taps - 1
        self.main = self.width - 128
        self.strip_rows = up(self.strip + 1 + self.field_halo, 8)
        self.fold = self.grad_pad // 2


def row_band_kernel(s, row_taps, weights, row_band, adj_high, adj_low, flipped):
    for f in range(s.filters):
        k, p = f // 2, f % 2
        pad = jnp.zeros((1, s.depth - s.taps), F32)
        row = jnp.concatenate([row_taps[k, p : p + 1, :], pad], 1)
        band = pltpu.roll(
            jnp.broadcast_to(row, (s.field_pad, s.depth)), 0, 1, stride=1, stride_axis=0
        )
        here = slice(f * s.field_pad, (f + 1) * s.field_pad)
        row_band[here, : s.depth], row_band[here, s.depth :] = split(band)
        flipped[here, :] = pltpu.roll(
            jnp.broadcast_to(row * (2.0 * weights[k : k + 1, :1]), (s.field_pad, s.depth)),
            s.depth - s.reach,
            1,
            stride=1,
            stride_axis=0,
        )
    turned = flipped[...].T[: s.grad_pad, :]
    adj_high[...], adj_low[...] = split(turned)


def col_band_kernel(s, col_taps, fwd_main, fwd_last, adj_main, adj_last):
    early = iota((128, 128), 1) < 128 - s.reach
    blocks = s.main // 128
    blank = jnp.zeros((128, 128), BF16)

    def fill(out, f, same, below):
        ends = split(jnp.where(early, same, 0.0))
        same, below = split(same), split(below)
        for part in range(2):
            for i in range(blocks):
                for j in range(blocks):
                    piece = blank
                    if i == j:
                        piece = ends[part] if j == blocks - 1 else same[part]
                    elif i == j + 1:
                        piece = below[part]
                    out[f, part, 128 * i : 128 * (i + 1), 128 * j : 128 * (j + 1)] = piece

    for f in range(s.filters):
        k, p = f // 2, f % 2
        pad = jnp.zeros((1, 256 - s.taps), F32)
        wide = jnp.concatenate([col_taps[k, p : p + 1, :], pad], 1)
        band = pltpu.roll(jnp.broadcast_to(wide, (128, 256)), 0, 1, stride=1, stride_axis=0)
        turned = band.T
        fill(fwd_main, f, turned[:128], turned[128:])
        corner = jnp.concatenate([band[: 128 - s.reach, :128], band[: s.reach, :128]], 0).T
        fwd_last[f, :, :128], fwd_last[f, :, 128:] = split(corner)
        band = pltpu.roll(
            jnp.broadcast_to(wide, (256, 256)), 256 - s.reach, 1, stride=1, stride_axis=0
        )[:, :128]
        fill(adj_main, f, band[:128], band[128:])
        corner = pltpu.roll(
            jnp.broadcast_to(wide[:, :128], (128, 128)), 128 - 2 * s.reach, 1, stride=1, stride_axis=0
        )
        adj_last[f, :, :128], adj_last[f, :, 128:] = split(corner)


def pulled_tile(value, start, lane):
    first = start // 128 * 128
    tile = value[:, first : first + 128]
    shift = (lane - start) % 128
    return pltpu.roll(tile, shift, 1) if shift else tile


def edge_kernel(
    s, listed_hbm, features_hbm, conv_weight_hbm, target_hbm, row_taps_hbm, col_taps_hbm, weights_hbm,
    table, acc, first_out, second_out, features, target, row_taps, col_taps, weights_out, own,
    listed, conv_weight, weights, sems,
):
    fetch = [
        pltpu.make_async_copy(conv_weight_hbm, conv_weight, sems.at[0]),
        pltpu.make_async_copy(listed_hbm, listed, sems.at[1]),
        pltpu.make_async_copy(target_hbm, target, sems.at[2]),
        pltpu.make_async_copy(row_taps_hbm, row_taps, sems.at[7]),
        pltpu.make_async_copy(col_taps_hbm, col_taps, sems.at[8]),
        pltpu.make_async_copy(weights_hbm, weights, sems.at[9]),
    ]
    slow = len(fetch)
    parts = 4
    rows = s.rows // parts
    for q in range(parts):
        here = pl.ds(q * rows, rows)
        fetch.append(
            pltpu.make_async_copy(features_hbm.at[:, here, :], features.at[:, here, :], sems.at[3 + q])
        )
    for copy in fetch:
        copy.start()
    acc[...] = jnp.zeros_like(acc)
    lanes = 128
    u, lane = iota((s.channels * ROWS, lanes), 0) % ROWS, iota((s.channels * ROWS, lanes), 1)
    h = lane % WIN
    owner = jnp.where(
        iota((s.channels * ROWS, s.channels), 0) // ROWS == iota((s.channels * ROWS, s.channels), 1), 1.0, 0.0
    ).astype(BF16)
    pick = jnp.where(iota((3, lanes), 1) // WIN == iota((3, lanes), 0), 1.0, 0.0)
    fetch[0].wait()
    flat = jnp.zeros((s.channels * ROWS, lanes), F32)
    for row_shift in range(3):
        spread = dot(conv_weight[row_shift].astype(F32), pick, ((0,), (0,))).astype(BF16)
        flat = jnp.where(h == u - row_shift + 2, dot(owner, spread), flat)
    table[...] = flat.astype(BF16)
    left = flat.T[: 3 * WIN].astype(BF16)
    for k in range(s.steps):
        if k % (s.steps // parts) == 0:
            fetch[slow + k // (s.steps // parts)].wait()
        block = features[:, k * ROWS : (k + 1) * ROWS, :].reshape(s.channels * ROWS, s.cols)
        for n in range(0, s.cols, 128):
            sums = dot(left, block[:, n : n + 128])
            for b in range(3):
                acc[b, k * ROWS : k * ROWS + WIN, n : n + 128] += sums[b * WIN : (b + 1) * WIN]
    for copy in fetch[1:slow]:
        copy.wait()
    for k in range(s.filters // 2):
        weights_out[k : k + 1, :] = jnp.broadcast_to(weights[k], (1, 128))
    across, down = s.cols // BLOCK, s.rows // BLOCK
    row, col = iota((8, s.width), 0), iota((8, s.width), 1) - s.mask_halo
    inside = (col >= 0) & (col < s.cols) & (row < down)
    number = jnp.where(inside, row * across + (col + BLOCK) // BLOCK - 1, -1)
    used = jnp.zeros((8, s.width), F32)
    for n in range(listed.shape[2]):
        used = jnp.where(number == listed[0, 0, n], 1.0, used)
    own[...] = used
    place, row = iota((s.grad_pad, 128), 1), iota((s.grad_pad, 128), 0)
    filler = jnp.zeros((s.grad_pad - s.rows, 128), F32)
    strips = []
    for first_aim, block_col in ((0, 0), (s.cols - s.field_halo, across - 1)):
        logits = jnp.zeros((s.grad_pad, 128), F32)
        for b in range(3):
            if block_col == 0:
                part = acc[b, : s.grad_pad, :128]
                shift, kept = 2 - b, place >= 2 - b
            else:
                part = acc[b, : s.grad_pad, s.cols - 128 :]
                shift, kept = s.strip - b, place < s.strip - b
            part = pltpu.roll(part, shift, 1) if shift else part
            logits += jnp.where(kept, part, 0.0)
        wanted = pulled_tile(target[...], first_aim, s.strip)
        wanted = jnp.concatenate([wanted, filler], 0)
        number = (row // BLOCK) * across + block_col
        used = jnp.zeros((s.grad_pad, 128), F32)
        for n in range(listed.shape[2]):
            used = jnp.where(number == listed[0, 0, n], 1.0, used)
        used = jnp.where(row < s.rows, used, 0.0)
        value = jnp.where(place < s.strip, logits, wanted)
        value = jnp.where(place < s.strip + s.field_halo, value, used)
        value = jnp.where(place < s.strip + s.field_halo + 1, value, 0.0)
        strips.append(
            jnp.where(iota((s.fold, 128), 1) < 64, value[: s.fold], pltpu.roll(value[s.fold :], 64, 1))
        )
    odd = neighbours("col")[2]
    first_out[...] = jnp.where(odd, strips[0], strips[1])
    second_out[...] = jnp.where(odd, strips[1], strips[0])


def partial_kernel(s, acc, partial):
    whole = jnp.zeros((s.grad_pad, s.width), F32)
    blank = jnp.zeros((s.grad_pad, s.width - s.cols), F32)
    for b in range(3):
        part = jnp.concatenate([acc[b, : s.grad_pad], blank], 1)
        whole += pltpu.roll(part, s.base + 2 - b, 1)
    partial[...] = whole


def unfolded(s, value):
    low = iota((s.fold, 128), 1) < 64
    return jnp.concatenate(
        [jnp.where(low, value, 0.0), jnp.where(low, pltpu.roll(value, 64, 1), 0.0)], 0
    )


def middle_kernel(s, own_used, partial, target, first, second, band, logits, aim, occupied, first_out, second_out):
    lane = iota((s.grad_pad, 128), 1)
    has_left, has_right, odd = neighbours("col")
    one, two = first[...], second[...]
    west = unfolded(s, jnp.where(has_left, jnp.where(odd, one, two), 0.0))
    east = unfolded(s, jnp.where(has_right, jnp.where(odd, two, one), 0.0))

    def placed(value, keep_from, keep, offset):
        kept = jnp.where((lane >= keep_from) & (lane < keep_from + keep), value, 0.0)
        shift = (offset - keep_from) % 128
        kept = pltpu.roll(kept, shift, 1) if shift else kept
        blank = jnp.zeros((s.grad_pad, 128), F32)
        return jnp.concatenate([kept if n == offset // 128 else blank for n in range(s.width // 128)], 1)

    whole = partial[...] + placed(west, 0, s.strip, 0)
    whole += placed(east, 0, s.strip, s.cols + s.base)
    logits[...] = whole
    own = jnp.concatenate([target[...], jnp.zeros((s.rows, s.width - s.cols), F32)], 1)
    aims = pltpu.roll(own, s.field_halo, 1)
    aims += placed(west, s.strip, s.field_halo, 0)[: s.rows]
    aims += placed(east, s.strip, s.field_halo, s.cols + s.field_halo)[: s.rows]
    aim[...] = aims

    down = s.rows // BLOCK
    row, col = iota((8, s.width), 0), iota((8, s.width), 1) - s.mask_halo
    used = own_used[...]
    flag = s.strip + s.field_halo
    for r in range(down):
        here = row == r
        used = jnp.where(here & (col < 0), west[r * BLOCK : r * BLOCK + 1, flag : flag + 1], used)
        beyond = here & (col >= s.cols) & (col < s.cols + s.mask_halo)
        used = jnp.where(beyond, east[r * BLOCK : r * BLOCK + 1, flag : flag + 1], used)
    occupied[...] = used

    odd = neighbours("row")[2]

    def fill(out, low):
        start = s.rows + 2 - s.strip if low else 0
        start_aim = s.rows - s.field_halo if low else 0
        block_row = down - 1 if low else 0
        out[...] = jnp.zeros_like(out)
        out[: s.strip, :] = whole[start : start + s.strip]
        out[s.strip : s.strip + 1, :] = used[block_row : block_row + 1]
        out[s.strip + 1 : s.strip + 1 + s.field_halo, :] = aims[start_aim : start_aim + s.field_halo]

    @pl.when(odd)
    def _():
        fill(first_out, False)
        fill(second_out, True)

    @pl.when(jnp.logical_not(odd))
    def _():
        fill(first_out, True)
        fill(second_out, False)


def overlapped(s, value):
    return jnp.concatenate([value[:, : s.main], pltpu.roll(value, s.reach, 1)[:, s.main :]], 1)


def optics_kernel(
    s, weights, logits, aim, occupied, first, second, row_band, fwd_main, fwd_last, adj_main, adj_last, adj_high, adj_low,
    features, shifted, exact, terms,
    ext, aims, masks, field, pulled, total,
):

    has_left, has_right, _ = neighbours("col")
    has_up, has_down, odd = neighbours("row")
    one, two = first[...], second[...]
    north = jnp.where(has_up, jnp.where(odd, one, two), 0.0)
    south = jnp.where(has_down, jnp.where(odd, two, one), 0.0)
    edge = up(s.strip, 8)
    lane_row = iota((edge, s.width), 0)
    ext[...] = jnp.zeros_like(ext)
    ext[s.base : s.base + s.grad_pad, :] = logits[...]
    ext[:edge, :] += jnp.where(lane_row < s.strip, north[:edge], 0.0)
    low = s.rows + s.base
    ext[low : low + edge, :] += jnp.where(lane_row < s.strip, south[:edge], 0.0)
    aims[...] = jnp.zeros_like(aims)
    aims[: s.field_halo, :] = north[s.strip + 1 : s.strip + 1 + s.field_halo]
    aims[s.field_halo : s.field_halo + s.rows, :] = aim[...]
    aims[s.field_halo + s.rows : s.field_rows, :] = south[s.strip + 1 : s.strip + 1 + s.field_halo]

    place = iota((s.mask_pad, s.width), 0) - s.mask_halo
    used = jnp.where(place < 0, north[s.strip : s.strip + 1], 0.0)
    for r in range(s.rows // BLOCK):
        used = jnp.where((place >= r * BLOCK) & (place < (r + 1) * BLOCK), occupied[r : r + 1, :], used)
    below = (place >= s.rows) & (place < s.rows + s.mask_halo)
    used = jnp.where(below, south[s.strip : s.strip + 1], used)
    sigma = jax.nn.sigmoid(ext[...])
    mask = used * sigma
    high, low = split(overlapped(s, mask))
    for first_row in (0, s.depth):
        here = slice(first_row, first_row + s.mask_pad)
        masks[here, : s.width] = high
        masks[here, s.width :] = low
        if s.mask_pad < s.depth:
            masks[first_row + s.mask_pad : first_row + s.depth, :] = jnp.zeros(
                (s.depth - s.mask_pad, 2 * s.width), BF16
            )
    slope = (mask * (1.0 - sigma))[s.base : s.base + s.grad_pad]
    slope = pltpu.roll(slope, s.width - s.base, 1)

    total[...] = jnp.zeros_like(total)
    group = 2
    tall = group * s.field_pad
    late = iota((s.field_pad, 128), 1) >= 128 - s.reach

    def banded(high, low, main, last):
        ends = jnp.concatenate([high[:, s.main :], low[:, s.main :]], 1)
        both = dot(ends, jnp.concatenate([last, last], 0))
        tail = both[:, :128] + both[:, 128:]
        high, low = high[:, : s.main], low[:, : s.main]
        rows = high.shape[0]
        both = dot(jnp.concatenate([high, low], 0), main[0])
        head = both[:rows] + both[rows:] + dot(high, main[1])
        seam = head[:, s.main - 128 :] + jnp.where(late, tail, 0.0)
        pieces = [seam, tail]
        if s.main > 128:
            pieces.insert(0, head[:, : s.main - 128])
        return jnp.concatenate(pieces, 1)

    for g in range(s.filters // group):
        band = row_band[g * tall : (g + 1) * tall, :]
        top, bottom = band[:, : s.depth], band[:, s.depth :]
        one = dot(top, masks[: s.depth, :])
        two = dot(bottom, masks[: s.depth, : s.width])
        rowed = one[:, : s.width] + one[:, s.width :] + two
        for i in range(0, group, 2):
            squares = 0.0
            for j in (i, i + 1):
                f = g * group + j
                high, low = split(rowed[j * s.field_pad : (j + 1) * s.field_pad])
                value = banded(high, low, fwd_main[f], fwd_last[f])
                field[f] = value
                squares += value * value
            k = (g * group + i) // 2
            total[...] += squares * weights[k : k + 1, :1]

    row, lane = iota((s.field_pad, s.width), 0) - s.field_halo, iota((s.field_pad, s.width), 1)
    col = jnp.where(lane < s.main, lane, lane - s.reach) - s.field_halo
    inside = ((row >= 0) | has_up) & ((row < s.rows) | has_down) & (row < s.rows + s.field_halo)
    inside &= ((col >= 0) | has_left) & ((col < s.cols) | has_right) & (col < s.cols + s.field_halo)
    total[...] = jnp.where(inside, total[...] - overlapped(s, aims[...]), 0.0)

    for f in range(s.filters):
        high, low = split(total[...] * field[f])
        high, low = split(banded(high, low, adj_main[f], adj_last[f]))
        rows = slice(f * s.field_pad, (f + 1) * s.field_pad)
        pulled[rows, : s.width] = high
        pulled[rows, s.width : s.width + 128] = low[:, s.main :]
        pulled[rows, s.width + 128 :] = low[:, : s.main]

    both = dot(jnp.concatenate([adj_high[...], adj_low[...]], 0), pulled[:, : s.width + 128])
    rest = both[: s.grad_pad, s.width :]
    both = both[: s.grad_pad, : s.width] + both[s.grad_pad :, : s.width]
    low = dot(adj_high[...], pulled[:, s.width + 128 :])
    grad = jnp.concatenate([both[:, : s.main] + low, both[:, s.main :] + rest], 1) * slope

    for b in range(3):
        moved = grad if b == 2 else pltpu.roll(grad, s.width - (2 - b), 1)
        shifted[b], shifted[3 + b] = split(moved[:, : s.cols])
    exact[...] = grad
    sums = jnp.zeros((s.channels * ROWS, 6 * WIN), F32)
    for k in range(s.steps):
        block = features[:, k * ROWS : (k + 1) * ROWS, :].reshape(s.channels * ROWS, s.cols)
        window = jnp.concatenate([shifted[q, k * ROWS : k * ROWS + WIN, :] for q in range(6)], 0)
        sums += dot(block, window, NT)
    cube = sums.reshape(s.channels, ROWS, 6 * WIN)
    u, lane = iota((ROWS, 6 * WIN), 0), iota((ROWS, 6 * WIN), 1)
    number, group = iota((16, 6 * WIN), 0), (iota((16, 6 * WIN), 1) // WIN) % 3
    result = jnp.zeros((16, s.channels), F32)
    for a in range(3):
        hit = jnp.where(lane % WIN == u - a + 2, 1.0, 0.0)
        line = (cube * hit[None]).sum(1)
        pick = jnp.where(number == a * 3 + group, 1.0, 0.0)
        result += dot(pick, line, NT, lax.Precision.HIGHEST)
    terms[...] = result


def feature_kernel(s, table, shifted, exact, out, blocks, third, sems):
    copies = []
    for b in range(3):
        moved = exact[...] if b == 2 else pltpu.roll(exact[...], s.width - (2 - b), 1)
        rest = moved[:, : s.cols] - shifted[b].astype(F32) - shifted[3 + b].astype(F32)
        third[b] = rest.astype(BF16)
    wide = jnp.concatenate([table[...]] * 3, 1)
    blank = jnp.zeros((WIN, s.cols), BF16)
    for k in range(s.steps):
        rows = slice(k * ROWS, k * ROWS + WIN)
        parts = []
        for part in range(3):
            parts += [(third[b, rows, :] if part == 2 else shifted[3 * part + b, rows, :]) for b in range(3)] + [blank]
        value = dot(wide, jnp.concatenate(parts, 0))
        here = pl.ds(k * ROWS, ROWS)
        blocks[:, here, :] = value.astype(BF16).reshape(s.channels, ROWS, s.cols)
        copies.append(pltpu.make_async_copy(blocks.at[:, here, :], out.at[:, here, :], sems.at[k]))
        copies[-1].start()
    for copy in copies:
        copy.wait()


def spec(space=pltpu.VMEM):
    return pl.BlockSpec(memory_space=space)


def exchanged(first, second, axis):
    size, parts = lax.axis_size(axis), lax.axis_size("grp")
    one = lax.ppermute(first, axis, [(i, i ^ 1) for i in range(size)])
    pairs = []
    for g in range(parts):
        for i in range(size):
            j = i + 1 if i % 2 else i - 1
            if 0 <= j < size:
                pairs.append((g * size + i, g * size + j))
            elif parts % 2:
                pairs.append((g * size + i, g * size + (j % size)))
            else:
                pairs.append((g * size + i, (g ^ 1) * size + i))
    return one, lax.ppermute(second, ("grp", axis), pairs)


def summed(value, axis):
    size = lax.axis_size(axis)
    parts = [
        lax.ppermute(value, axis, [(i, i ^ step) for i in range(size)]) for step in range(1, size)
    ]
    return functools.reduce(jnp.add, parts, value)


def on_device(features, conv_weight, row_taps, col_taps, kernel_weight, target, block_list):
    channels, tile_rows, tile_cols = features.shape
    s = Sizes(channels, tile_rows, tile_cols, row_taps.shape[2], row_taps.shape[0] * 2)
    shape = jax.ShapeDtypeStruct
    hbm = spec(pltpu.HBM)

    def call(body, outs, ins, scratch=(), limit=24, out_space=pltpu.VMEM):
        return pl.pallas_call(
            functools.partial(body, s),
            out_shape=outs,
            in_specs=ins,
            out_specs=jax.tree.map(lambda _: spec(out_space), outs),
            scratch_shapes=list(scratch),
            compiler_params=pltpu.CompilerParams(vmem_limit_bytes=limit * MIB),
        )

    half_strip = shape((s.fold, 128), F32)
    table, sums, first, second, features_here, target_here, row_here, col_here, weights, own = call(
        edge_kernel,
        (
            shape((channels * ROWS, 128), BF16),
            shape((3, s.rows + WIN, s.cols), F32),
            half_strip,
            half_strip,
            shape(features.shape, BF16),
            shape(target.shape, F32),
            shape(row_taps.shape, F32),
            shape(col_taps.shape, F32),
            shape((8 * -(-s.filters // 16), 128), F32),
            shape((8, s.width), F32),
        ),
        [hbm] * 7,
        [
            pltpu.SMEM(block_list.shape, jnp.int32),
            pltpu.VMEM((3, 3, channels), BF16),
            pltpu.SMEM(kernel_weight.shape, F32),
            pltpu.SemaphoreType.DMA((10,)),
        ],
    )(
        *(
            pltpu.with_memory_space_constraint(x, pltpu.HBM)
            for x in (
                block_list, features, conv_weight.transpose(1, 2, 0), target, row_taps, col_taps,
                kernel_weight,
            )
        )
    )
    first, second = exchanged(first, second, "col")
    partial = call(partial_kernel, shape((s.grad_pad, s.width), F32), [spec()])(sums)

    filters = s.filters
    col_bands = call(
        col_band_kernel,
        (shape((filters, 2, s.main, s.main), BF16), shape((filters, 128, 256), BF16)) * 2,
        [spec()],
    )(col_here)
    row_bands = call(
        row_band_kernel,
        (
            shape((filters * s.field_pad, 2 * s.depth), BF16),
            shape((s.grad_pad, filters * s.field_pad), BF16),
            shape((s.grad_pad, filters * s.field_pad), BF16),
        ),
        [spec(), spec()],
        [pltpu.VMEM((filters * s.field_pad, s.depth), F32)],
    )(row_here, weights)

    row_strip = shape((s.strip_rows, s.width), F32)
    logits, aim, occupied, first, second = call(
        middle_kernel,
        (
            shape((s.grad_pad, s.width), F32),
            shape((s.rows, s.width), F32),
            shape((8, s.width), F32),
            row_strip,
            row_strip,
        ),
        [spec()] * 6,
    )(own, partial, target_here, first, second, col_bands[1])
    first, second = exchanged(first, second, "row")

    shifted, exact, terms = call(
        optics_kernel,
        (shape((6, s.grad_pad, s.cols), BF16), shape((s.grad_pad, s.width), F32), shape((16, channels), F32)),
        [spec()] * 14,
        [
            pltpu.VMEM((s.mask_pad, s.width), F32),
            pltpu.VMEM((s.field_pad, s.width), F32),
            pltpu.VMEM((2 * s.depth, 2 * s.width), BF16),
            pltpu.VMEM((filters, s.field_pad, s.width), F32),
            pltpu.VMEM((filters * s.field_pad, 2 * s.width), BF16),
            pltpu.VMEM((s.field_pad, s.width), F32),
        ],
        32,
    )(weights, logits, aim, occupied, first, second, *row_bands[:1], *col_bands, *row_bands[1:], features_here)

    by_row = summed(terms, "row")
    grad_features = call(
        feature_kernel,
        shape(features.shape, BF16),
        [spec()] * 3,
        [
            pltpu.VMEM(features.shape, BF16),
            pltpu.VMEM((3, s.grad_pad, s.cols), BF16),
            pltpu.SemaphoreType.DMA((s.steps,)),
        ],
        out_space=pltpu.HBM,
    )(table, shifted, exact)
    whole = summed(by_row, "col")
    height = tile_rows * lax.axis_size("row")
    width = tile_cols * lax.axis_size("col")
    grad_weight = (whole[:9].T / math.sqrt(height * width)).reshape(channels, 3, 3)
    return (grad_weight, grad_features)


def solution(mesh):
    placed = (
        P(None, ("grp", "row"), "col"),
        P(),
        P(),
        P(),
        P(),
        P(("grp", "row"), "col"),
        P(("grp", "row"), "col", None),
    )
    return jax.shard_map(
        on_device,
        mesh=mesh,
        in_specs=placed,
        out_specs=(P("grp", None, None), P(None, ("grp", "row"), "col")),
        check_vma=False,
    )
```
